32 devices in a mesh: tm: 4 (over x, core), space: 8 (over z, y).
Axes of the slice: x: 2, y: 2, z: 4, core: 2. Of those that a mesh axis runs over, the one named last changes fastest.
Arguments:
- frames_in: bfloat16 [24, 64, 128, 128], P('tm', 'space'), may hold values from -6 to 6
- boundary: bfloat16 [5, 2, 128, 128], replicated, may hold values from -6 to 6
- conv_first: bfloat16 [3, 3, 128, 128], replicated, may hold values from -0.1875 to 0.1875
- conv_second: bfloat16 [3, 3, 128, 128], replicated, may hold values from -0.1875 to 0.1875
- norm_gain: float32 [128], replicated, may hold values from 0.1 to 1.9
- qkv_weight: bfloat16 [128, 384], replicated, as said below
- out_weight: bfloat16 [128, 128], replicated, may hold values from -0.5 to 0.5
Outputs:
- block_out: bfloat16 [24, 64, 128, 128], P('tm', 'space')
The draws below stay inside these ranges and needn't reach their ends.
Inputs may be any that keep to these rules, and one draw needn't show every extreme that they name: `qkv_weight`: a projection matrix.
All inputs are finite; a program needn't handle non-finite values.
Results may differ from the reference program's by a relative error of at most 0.034.
The reference program's roundings to bfloat16 on the way count: a program that leaves them out, or rounds other values in their place, can miss the bound.
Values may be sent and summed in bfloat16 or wider, within the bound.
A program may use at most 128 MiB of HBM per device.

```python
import math
import jax
import jax.numpy as jnp
from jax import lax

CH = 128
HEADS = 8
FRAMES = 24
COARSE = 5
COLS = 128
ROWS = 64


def draw_qkv_weight(key, part):
    base = jax.random.normal(key, (CH, 3 * CH), jnp.float32)
    factor = 1.0
    return (jnp.clip(base, -4.0, 4.0) * (factor / math.sqrt(CH))).astype(jnp.bfloat16)


def block_levels(own_key, extent, cuts, least, largest):
    def one(position, blocks):
        draws = jax.random.uniform(jax.random.fold_in(jax.random.fold_in(own_key, 6), position), (blocks,), jnp.float32, least / len(cuts), largest / len(cuts))
        return jnp.repeat(jnp.exp(draws), extent[position] // blocks).reshape((-1,) + (1,) * (len(extent) - position - 1))

    factor_of = one(*cuts[0])
    for cut in cuts[1:]:
        factor_of = factor_of * one(*cut)
    return factor_of


def normal_values(own_key, shape, scale, bound, cuts=(), kind=jnp.bfloat16):
    level = block_levels(own_key, shape, cuts, -0.22, 0.18) if cuts else 1.0
    result = jax.random.normal(own_key, shape, jnp.float32) * scale * level
    return jnp.minimum(jnp.maximum(result, -bound), bound).astype(kind)


def setup_inputs(seed: int = 0) -> dict:
    streams_of = jax.random.split(jax.random.key(seed), 8)
    frames_in = normal_values(streams_of[0], (FRAMES, ROWS, COLS, CH), 1.0, 6.0, ((0, 4), (1, 8)))
    boundary = normal_values(streams_of[1], (COARSE, 2, COLS, CH), 1.0, 6.0)
    conv_first = normal_values(streams_of[2], (3, 3, CH, CH), (9 * CH) ** -0.5, 0.1875)
    conv_second = normal_values(streams_of[3], (3, 3, CH, CH), (9 * CH) ** -0.5, 0.1875)
    norm_gain = jnp.clip(1.0 + 0.18 * jax.random.normal(streams_of[4], (CH,), jnp.float32), 0.1, 1.9)
    qkv_weight = draw_qkv_weight(jax.random.fold_in(streams_of[7], 71), 0)
    out_weight = normal_values(streams_of[6], (CH, CH), CH ** -0.5, 0.5)
    return {"frames_in": frames_in, "boundary": boundary, "conv_first": conv_first, "conv_second": conv_second, "norm_gain": norm_gain, "qkv_weight": qkv_weight, "out_weight": out_weight}


def interp_matrix(times):
    scaled = times * (COARSE - 1)
    lower = scaled // (FRAMES - 1)
    upper = jnp.minimum(lower + 1, COARSE - 1)
    frac = (scaled - lower * (FRAMES - 1)).astype(jnp.float32) / float(FRAMES - 1)
    levels = jnp.arange(COARSE, dtype=jnp.int32)
    low_hot = (levels[None, :] == lower[:, None]).astype(jnp.float32)
    up_hot = (levels[None, :] == upper[:, None]).astype(jnp.float32)
    return (1.0 - frac)[:, None] * low_hot + frac[:, None] * up_hot

def conv_frame(padded, kernel):
    rows = padded.shape[0] - 2
    width = padded.shape[1] - 2
    chans = padded.shape[2]
    total = jnp.zeros((rows * width, kernel.shape[3]), jnp.float32)
    for shift_r in range(3):
        for shift_c in range(3):
            piece = padded[shift_r:shift_r + rows, shift_c:shift_c + width].reshape(rows * width, chans)
            total = total + jnp.dot(piece, kernel[shift_r, shift_c], preferred_element_type=jnp.float32)
    return total.reshape(rows, width, kernel.shape[3])

def extend_frame(frame, strip):
    rows = jnp.concatenate([strip[0:1], frame, strip[1:2]], axis=0)
    return jnp.pad(rows, ((0, 0), (1, 1), (0, 0)))

def temporal(resid, norm_gain, qkv_weight, out_weight):
    nframes, pixels, chans = resid.shape
    head_dim = chans // HEADS
    rf = resid.astype(jnp.float32)
    normed = (rf * lax.rsqrt(lax.optimization_barrier(jnp.mean(rf * rf, axis=-1, keepdims=True)) + 1e-06) * norm_gain).astype(jnp.bfloat16)
    qkv = jnp.dot(normed.reshape(nframes * pixels, chans), qkv_weight, preferred_element_type=jnp.float32)
    qkv = qkv.astype(jnp.bfloat16).reshape(nframes, pixels, 3, HEADS, head_dim)
    query = qkv[:, :, 0].astype(jnp.float32)
    key_part = qkv[:, :, 1].astype(jnp.float32)
    value = qkv[:, :, 2].astype(jnp.float32)
    scores = jnp.einsum('fphd,gphd->phfg', query, key_part) * (1.0 / head_dim ** 0.5)
    top = lax.optimization_barrier(jnp.max(scores, axis=-1, keepdims=True))
    expd = jnp.exp(scores - top)
    probs = (expd / lax.optimization_barrier(jnp.sum(expd, axis=-1, keepdims=True))).astype(jnp.bfloat16)
    attended = jnp.einsum('phfg,gphd->fphd', probs.astype(jnp.float32), value).astype(jnp.bfloat16)
    proj = jnp.dot(attended.reshape(nframes * pixels, chans), out_weight, preferred_element_type=jnp.float32)
    return (rf.reshape(nframes * pixels, chans) + proj).astype(jnp.bfloat16).reshape(nframes, pixels, chans)

def reference(frames_in, boundary, conv_first, conv_second, norm_gain, qkv_weight, out_weight):
    times = jnp.arange(FRAMES, dtype=jnp.int32)
    weights = interp_matrix(times)
    strips = jnp.einsum('tk,kscx->tscx', weights, boundary.astype(jnp.float32)).astype(jnp.bfloat16)

    def one_frame(pair):
        frame, strip = pair
        first = conv_frame(extend_frame(frame, strip), conv_first)
        hidden = jax.nn.silu(first).astype(jnp.bfloat16)
        second = conv_frame(extend_frame(hidden, strip), conv_second)
        return (frame.astype(jnp.float32) + second).astype(jnp.bfloat16)
    resid = lax.map(one_frame, (frames_in, strips))
    by_rows = jnp.swapaxes(resid, 0, 1)

    def one_row(row_block):
        return temporal(row_block, norm_gain, qkv_weight, out_weight)
    mixed = lax.map(one_row, by_rows)
    return jnp.swapaxes(mixed, 0, 1)
```

```python
import functools

import jax
import jax.numpy as jnp
from jax import lax
from jax.experimental import pallas as pl
from jax.experimental.pallas import tpu as pltpu
from jax.sharding import PartitionSpec as P

HEADS = 8
MESH = pl.DeviceIdType.MESH
CELLS = 32
GROUP = 8


def conv_taps(taps, weight, width):
    cells = jnp.concatenate(taps, axis=1)
    rows = cells.shape[0]
    chans = weight.shape[1] // 3
    wide = jnp.dot(cells, weight, preferred_element_type=jnp.float32)
    col = lax.rem(lax.broadcasted_iota(jnp.int32, (rows, chans), 0), width)
    left = jnp.where(col == 0, 0.0, pltpu.roll(wide[:, :chans], 1, 0))
    right = jnp.where(col == width - 1, 0.0, pltpu.roll(wide[:, 2 * chans :], rows - 1, 0))
    return wide[:, chans : 2 * chans] + left + right


def attend(normed, resid, qkv_weight, out_weight, mask, heads_of):
    nframes, cells, chans = normed.shape
    mine = resid.shape[0]
    head_dim = chans // HEADS
    keys = nframes * GROUP
    asks = mine * GROUP
    query = jnp.dot(
        normed[:mine].reshape(mine * cells, chans), qkv_weight[:, :chans], preferred_element_type=jnp.float32
    ).reshape(mine, cells, chans)
    kv = jnp.dot(
        normed.reshape(nframes * cells, chans), qkv_weight[:, chans:], preferred_element_type=jnp.float32
    ).reshape(nframes, cells, 2 * chans)
    outs, kept = [], []
    for j in range(0, cells, GROUP):
        part = query[:, j : j + GROUP].reshape(asks, chans).astype(jnp.bfloat16)
        part = part * jnp.bfloat16(1.0 / head_dim**0.5)
        pair = kv[:, j : j + GROUP].reshape(keys, 2 * chans).astype(jnp.bfloat16)
        key_part, value = pair[:, :chans], pair[:, chans:]
        with_ones = jnp.concatenate([value, jnp.ones_like(value)], axis=1)
        picked = jnp.concatenate(
            [jnp.where(heads_of == h, part, jnp.zeros_like(part)) for h in range(HEADS)], axis=0
        )
        scores = lax.dot_general(
            picked, key_part, (((1,), (1,)), ((), ())), preferred_element_type=jnp.float32
        )
        scores = (scores.reshape(HEADS, asks, keys) + mask).reshape(HEADS * asks, keys)
        top = jnp.max(scores, axis=-1, keepdims=True)
        expd = jnp.exp((scores - top).astype(jnp.bfloat16))
        both = jnp.dot(expd, with_ones, preferred_element_type=jnp.float32)
        num, den = both[:asks, :chans], both[:asks, chans:]
        for h in range(1, HEADS):
            piece = both[h * asks : (h + 1) * asks]
            own = heads_of == h
            num = jnp.where(own, piece[:, :chans], num)
            den = jnp.where(own, piece[:, chans:], den)
        outs.append((num / den).astype(jnp.bfloat16))
        kept.append(resid[:, j : j + GROUP].reshape(asks, chans))
    attended = jnp.concatenate(outs, axis=0)
    out = jnp.concatenate(kept, axis=0) + jnp.dot(attended, out_weight, preferred_element_type=jnp.float32)
    parts = [out[g * asks : (g + 1) * asks].reshape(mine, GROUP, chans) for g in range(cells // GROUP)]
    return jnp.concatenate(parts, axis=1)


def block_kernel(
    peers, spaces,
    x_ref, boundary_ref, w1_ref, w2_ref, gain_ref, qkv_hbm, outw_hbm, o_ref,
    xpad, hpad, rbuf, nbuf, nall, rsib, abuf, wcat, bnd, qkv_ref, outw_ref, mask_ref,
    x_sem, w_sem, b_sem, p_sem, halo_send, halo_recv, early_send, early_recv, there_send, there_recv,
    back_send, back_recv,
):
    nloc, rows, width, chans = x_ref.shape
    coarse = boundary_ref.shape[0]
    nframes = nloc * peers
    half = width // 2
    me = lax.axis_index("tm")
    place = lax.axis_index("space")
    last = spaces - 1
    core = lax.rem(me, 2)
    base = me - core
    other = lax.rem(base + 2, peers)
    peer = (me, base + 1 - core, other + core, other + 1 - core)
    half_of = (core, 1 - core, core, 1 - core)

    loads = [pltpu.make_async_copy(x_ref.at[f], xpad.at[f, pl.ds(2, rows)], x_sem.at[f]) for f in range(nloc)]
    weights = [
        pltpu.make_async_copy(
            ref.at[dy, dx],
            wcat.at[which, pl.ds(dy * chans, chans), pl.ds(dx * chans, chans)],
            w_sem.at[which, 3 * dy + dx],
        )
        for which, ref in enumerate((w1_ref, w2_ref))
        for dy in range(3)
        for dx in range(3)
    ]
    edges = pltpu.make_async_copy(boundary_ref, bnd, b_sem)
    projections = [
        pltpu.make_async_copy(qkv_hbm, qkv_ref, p_sem.at[0]),
        pltpu.make_async_copy(outw_hbm, outw_ref, p_sem.at[1]),
    ]
    loads[0].start()
    for w in weights:
        w.start()
    for x in loads[1:]:
        x.start()
    for p in projections:
        p.start()
    edges.start()

    barrier = pltpu.get_barrier_semaphore()
    for k in range(1, 4):
        pl.semaphore_signal(barrier, inc=1, device_id={"tm": peer[k]}, device_id_type=MESH)

    @pl.when(place > 0)
    def _():
        pl.semaphore_signal(barrier, inc=1, device_id={"space": place - 1}, device_id_type=MESH)

    @pl.when(place < last)
    def _():
        pl.semaphore_signal(barrier, inc=1, device_id={"space": place + 1}, device_id_type=MESH)

    beside = jnp.where(place > 0, 1, 0) + jnp.where(place < last, 1, 0)
    pl.semaphore_wait(barrier, 3 + beside)

    def up(i):
        return pltpu.make_async_remote_copy(
            x_ref.at[:, i], xpad.at[:, rows + 2 + i], halo_send.at[0, i], halo_recv.at[0, i],
            device_id={"space": place - 1}, device_id_type=MESH,
        )

    def down(i):
        return pltpu.make_async_remote_copy(
            x_ref.at[:, rows - 1 - i], xpad.at[:, 1 - i], halo_send.at[1, i], halo_recv.at[1, i],
            device_id={"space": place + 1}, device_id_type=MESH,
        )

    @pl.when(place > 0)
    def _():
        up(0).start()
        up(1).start()

    @pl.when(place < last)
    def _():
        down(0).start()
        down(1).start()

    row_id = lax.broadcasted_iota(jnp.int32, mask_ref.shape, 0)
    col_id = lax.broadcasted_iota(jnp.int32, mask_ref.shape, 1)
    mask_ref[...] = jnp.where(lax.rem(row_id, GROUP) == lax.rem(col_id, GROUP), 0.0, -1e30)
    heads_of = lax.broadcasted_iota(jnp.int32, (2 * nloc * GROUP, chans), 1) // (chans // HEADS)
    gain = gain_ref[...]

    def strip(frame, side):
        scaled = (me * nloc + frame) * (coarse - 1)
        lower = scaled // (nframes - 1)
        upper = jnp.minimum(lower + 1, coarse - 1)
        frac = (scaled - lower * (nframes - 1)).astype(jnp.float32) / float(nframes - 1)
        low, high = bnd[lower, side].astype(jnp.float32), bnd[upper, side].astype(jnp.float32)
        return ((1.0 - frac) * low + frac * high).astype(jnp.bfloat16)

    def stacked(ref, frame, which):
        return jnp.concatenate([ref[frame, r] for r in which], axis=0)

    def hidden_rows(frame, which):
        taps = [stacked(xpad, frame, [r + dy for r in which]) for dy in range(3)]
        first = conv_taps(taps, wcat[0], width)
        act = (first / (1.0 + jnp.exp(-first))).astype(jnp.bfloat16)
        for i, r in enumerate(which):
            hpad[frame, r] = act[i * width : (i + 1) * width]

    def resid_rows(frame, which, slot):
        taps = [stacked(hpad, frame, [r + dy for r in which]) for dy in range(3)]
        second = conv_taps(taps, wcat[1], width)
        before = stacked(xpad, frame, [r + 2 for r in which])
        resid = (before.astype(jnp.float32) + second).astype(jnp.bfloat16)
        wide = resid.astype(jnp.float32)
        mean_sq = jnp.mean(wide * wide, axis=-1, keepdims=True)
        normed = (wide * lax.rsqrt(mean_sq + 1e-06) * gain).astype(jnp.bfloat16)
        for i in range(len(which)):
            rbuf[slot + i, frame] = resid[i * width : (i + 1) * width]
            nbuf[slot + i, frame] = normed[i * width : (i + 1) * width]

    def early(frame, k):
        to = 1 if k == 4 else k
        cols = pl.ds(pl.multiple_of(half_of[to] * half, half), half)
        src = (rbuf if k == 4 else nbuf).at[0, frame, cols]
        dst = rsib.at[0, frame] if k == 4 else nall.at[0, k - 1, frame]
        return pltpu.make_async_remote_copy(
            src, dst, early_send.at[frame, k - 1], early_recv.at[frame, k - 1],
            device_id={"tm": peer[to]}, device_id_type=MESH,
        )

    def there(slot, part, k):
        to = 1 if k == 4 else k
        begin = part * CELLS
        cols = pl.ds(pl.multiple_of(half_of[to] * half + begin, CELLS), CELLS)
        here = pl.ds(pl.multiple_of(begin, CELLS), CELLS)
        src = (rbuf if k == 4 else nbuf).at[slot, :, cols]
        dst = rsib.at[slot, :, here] if k == 4 else nall.at[slot, k - 1, :, here]
        return pltpu.make_async_remote_copy(
            src, dst, there_send.at[slot, part, k - 1], there_recv.at[slot, part, k - 1],
            device_id={"tm": peer[to]}, device_id_type=MESH,
        )

    order = (2, 3, 1, 4)
    parts = half // CELLS

    def send_slot(slot):
        for part in range(parts):
            for k in order:
                there(slot, part, k).start()

    for w in weights:
        w.wait()

    for x in loads[:1]:
        x.wait()

    def first_pair(frame, carry):
        hidden_rows(frame, [2, 3, 4, 5])
        resid_rows(frame, [2, 3], 0)
        for k in order:
            early(frame, k).start()
        return carry

    first_pair(0, 0)
    for x in loads[1:]:
        x.wait()
    lax.fori_loop(1, nloc, first_pair, 0)
    send_slot(1)

    def inner_pair(frame, carry):
        hidden_rows(frame, [6, 7])
        resid_rows(frame, [4, 5], 2)
        return carry

    lax.fori_loop(0, nloc, inner_pair, 0)
    send_slot(2)
    send_slot(3)

    for p in projections:
        p.wait()
    edges.wait()

    def near_pair():
        @pl.when(place > 0)
        def _():
            down(0).wait_recv()

        @pl.when(place == 0)
        def _():
            for f in range(nloc):
                edge = strip(f, 0)
                xpad[f, 0] = edge
                xpad[f, 1] = edge

        @pl.when(place < last)
        def _():
            up(0).wait_recv()

        @pl.when(place == last)
        def _():
            for f in range(nloc):
                edge = strip(f, 1)
                xpad[f, rows + 2] = edge
                xpad[f, rows + 3] = edge

        def one(frame, carry):
            hidden_rows(frame, [1, rows])
            resid_rows(frame, [1, rows - 2], 4)
            return carry

        lax.fori_loop(0, nloc, one, 0)
        send_slot(4)
        send_slot(5)

    def edge_pair():
        @pl.when(place > 0)
        def _():
            down(1).wait_recv()

        @pl.when(place < last)
        def _():
            up(1).wait_recv()

        def one(frame, carry):
            hidden_rows(frame, [0, rows + 1])
            return carry

        lax.fori_loop(0, nloc, one, 0)

        @pl.when(place == 0)
        def _():
            hpad[:, 0] = xpad[:, 1]

        @pl.when(place == last)
        def _():
            hpad[:, rows + 1] = xpad[:, rows + 2]

        def two(frame, carry):
            resid_rows(frame, [0, rows - 1], 6)
            return carry

        lax.fori_loop(0, nloc, two, 0)
        send_slot(6)
        send_slot(7)

    def row_of(slot):
        k = slot - 4
        far = lax.rem(k + 4, 2)
        outer = (1 - k // 2) * (1 - far) + (rows - 2 + k // 2) * far
        return jnp.where(slot < 4, slot + 2, outer)

    def back(slot, part):
        here = pl.ds(pl.multiple_of(part * CELLS, CELLS), CELLS)
        cols = pl.ds(pl.multiple_of(core * half + part * CELLS, CELLS), CELLS)
        return pltpu.make_async_remote_copy(
            abuf.at[slot, :, here], o_ref.at[:, row_of(slot), cols],
            back_send.at[slot, part], back_recv.at[slot, part],
            device_id={"tm": peer[1]}, device_id_type=MESH,
        )

    for f in range(nloc):
        for k in order:
            early(f, k).wait_recv()

    def step(s, carry):
        slot = s // parts
        part = lax.rem(s, parts)

        @pl.when(slot > 0)
        def _():
            for k in order:
                there(slot, part, k).wait_recv()

        here = pl.ds(pl.multiple_of(part * CELLS, CELLS), CELLS)
        cols = pl.ds(pl.multiple_of(core * half + part * CELLS, CELLS), CELLS)
        normed = jnp.concatenate(
            [nbuf[slot, :, cols, :], nall[slot, :, :, here, :].reshape(3 * nloc, CELLS, chans)], axis=0
        )
        resid = jnp.concatenate([rbuf[slot, :, cols, :], rsib[slot, :, here, :]], axis=0).astype(jnp.float32)
        out = attend(normed, resid, qkv_ref[...], outw_ref[...], mask_ref[...], heads_of).astype(jnp.bfloat16)
        abuf[slot, :, here, :] = out[nloc:]
        back(slot, part).start()
        o_ref[:, row_of(slot), cols, :] = out[:nloc]

        @pl.when(s == parts - 1)
        def _():
            near_pair()

        @pl.when(s == 3 * parts - 1)
        def _():
            edge_pair()

        return carry

    lax.fori_loop(0, rows * parts, step, 0)

    @pl.when(place > 0)
    def _():
        up(0).wait_send()
        up(1).wait_send()

    @pl.when(place < last)
    def _():
        down(0).wait_send()
        down(1).wait_send()

    for f in range(nloc):
        for k in order:
            early(f, k).wait_send()

    def drain(slot, carry):
        for part in range(parts):
            for k in order:
                there(slot, part, k).wait_send()
        return carry

    lax.fori_loop(1, rows, drain, 0)

    def settle(slot, carry):
        for part in range(parts):
            back(slot, part).wait()
        return carry

    lax.fori_loop(0, rows, settle, 0)


def on_device(frames_in, boundary, conv_first, conv_second, norm_gain, qkv_weight, out_weight):
    nloc, rows, width, chans = frames_in.shape
    peers = lax.axis_size("tm")
    spaces = lax.axis_size("space")
    nframes = nloc * peers
    half = width // 2
    parts = half // CELLS
    vmem = pl.BlockSpec(memory_space=pltpu.VMEM)
    hbm = pl.BlockSpec(memory_space=pl.ANY)
    bf16 = jnp.bfloat16
    dma = pltpu.SemaphoreType.DMA
    return pl.pallas_call(
        functools.partial(block_kernel, peers, spaces),
        out_shape=jax.ShapeDtypeStruct(frames_in.shape, frames_in.dtype),
        in_specs=[hbm] * 4 + [vmem] + [hbm] * 2,
        out_specs=vmem,
        scratch_shapes=[
            pltpu.VMEM((nloc, rows + 4, width, chans), bf16),
            pltpu.VMEM((nloc, rows + 2, width, chans), bf16),
            pltpu.VMEM((rows, nloc, width, chans), bf16),
            pltpu.VMEM((rows, nloc, width, chans), bf16),
            pltpu.VMEM((rows, peers - 1, nloc, half, chans), bf16),
            pltpu.VMEM((rows, nloc, half, chans), bf16),
            pltpu.VMEM((rows, nloc, half, chans), bf16),
            pltpu.VMEM((2, 3 * chans, 3 * chans), bf16),
            pltpu.VMEM(boundary.shape, bf16),
            pltpu.VMEM(qkv_weight.shape, bf16),
            pltpu.VMEM(out_weight.shape, bf16),
            pltpu.VMEM((2 * nloc * GROUP, nframes * GROUP), jnp.float32),
            dma((nloc,)), dma((2, 9)), dma, dma((2,)), dma((2, 2)), dma((2, 2)),
            dma((nloc, 4)), dma((nloc, 4)), dma((rows, parts, 4)), dma((rows, parts, 4)),
            dma((rows, parts)), dma((rows, parts)),
        ],
        compiler_params=pltpu.CompilerParams(
            collective_id=0, has_side_effects=True, vmem_limit_bytes=56 * 1024 * 1024
        ),
        name="denoise",
    )(frames_in, boundary, conv_first, conv_second, norm_gain.reshape(1, chans), qkv_weight, out_weight)


def solution(mesh):
    placed = (P("tm", "space", None, None), P(), P(), P(), P(), P(), P())
    return jax.shard_map(
        on_device,
        mesh=mesh,
        in_specs=placed,
        out_specs=P("tm", "space", None, None),
        check_vma=False,
    )
```

```python
import functools

import jax
import jax.numpy as jnp
from jax import lax
from jax.experimental import pallas as pl
from jax.experimental.pallas import tpu as pltpu
from jax.sharding import PartitionSpec as P

HEADS = 8
MESH = pl.DeviceIdType.MESH
CELLS = 64
GROUP = 8
BATCH = 3


def conv_taps(taps, weight, width):
    cells = jnp.concatenate(taps, axis=1)
    rows = cells.shape[0]
    chans = weight.shape[1] // 3
    wide = jnp.dot(cells, weight, preferred_element_type=jnp.float32)
    col = lax.rem(lax.broadcasted_iota(jnp.int32, (rows, chans), 0), width)
    left = jnp.where(col == 0, 0.0, pltpu.roll(wide[:, :chans], 1, 0))
    right = jnp.where(col == width - 1, 0.0, pltpu.roll(wide[:, 2 * chans :], rows - 1, 0))
    return wide[:, chans : 2 * chans] + left + right


def attend(normed, resid, qkv_weight, out_weight, mask, heads_of):
    nframes, cells, chans = normed.shape
    mine = resid.shape[0]
    head_dim = chans // HEADS
    keys = nframes * GROUP
    asks = mine * GROUP
    query = jnp.dot(
        normed[:mine].reshape(mine * cells, chans), qkv_weight[:, :chans], preferred_element_type=jnp.float32
    ).reshape(mine, cells, chans)
    kv = jnp.dot(
        normed.reshape(nframes * cells, chans), qkv_weight[:, chans:], preferred_element_type=jnp.float32
    ).reshape(nframes, cells, 2 * chans)
    outs, kept = [], []
    for j in range(0, cells, GROUP):
        part = query[:, j : j + GROUP].reshape(asks, chans).astype(jnp.bfloat16)
        part = part * jnp.bfloat16(1.0 / head_dim**0.5)
        pair = kv[:, j : j + GROUP].reshape(keys, 2 * chans).astype(jnp.bfloat16)
        key_part, value = pair[:, :chans], pair[:, chans:]
        with_ones = jnp.concatenate([value, jnp.ones_like(value)], axis=1)
        picked = jnp.concatenate(
            [jnp.where(heads_of == h, part, jnp.zeros_like(part)) for h in range(HEADS)], axis=0
        )
        scores = lax.dot_general(
            picked, key_part, (((1,), (1,)), ((), ())), preferred_element_type=jnp.float32
        )
        scores = (scores.reshape(HEADS, asks, keys) + mask).reshape(HEADS * asks, keys)
        top = jnp.max(scores, axis=-1, keepdims=True)
        expd = jnp.exp((scores - top).astype(jnp.bfloat16))
        both = jnp.dot(expd, with_ones, preferred_element_type=jnp.float32)
        num, den = both[:asks, :chans], both[:asks, chans:]
        for h in range(1, HEADS):
            piece = both[h * asks : (h + 1) * asks]
            own = heads_of == h
            num = jnp.where(own, piece[:, :chans], num)
            den = jnp.where(own, piece[:, chans:], den)
        outs.append((num / den).astype(jnp.bfloat16))
        kept.append(resid[:, j : j + GROUP].reshape(asks, chans))
    attended = jnp.concatenate(outs, axis=0)
    out = jnp.concatenate(kept, axis=0) + jnp.dot(attended, out_weight, preferred_element_type=jnp.float32)
    parts = [out[g * asks : (g + 1) * asks].reshape(mine, GROUP, chans) for g in range(cells // GROUP)]
    return jnp.concatenate(parts, axis=1)


def block_kernel(
    peers, spaces,
    x_ref, boundary_ref, w1_ref, w2_ref, gain_ref, qkv_hbm, outw_hbm, o_ref,
    xpad, hpad, rbuf, nbuf, nall, rsib, abuf, wcat, bnd, qkv_ref, outw_ref, mask_ref,
    x_sem, w_sem, b_sem, p_sem, halo_send, halo_recv, early_send, early_recv, there_send, there_recv,
    back_send, back_recv,
):
    nloc, rows, width, chans = x_ref.shape
    coarse = boundary_ref.shape[0]
    nframes = nloc * peers
    half = width // 2
    me = lax.axis_index("tm")
    place = lax.axis_index("space")
    last = spaces - 1
    core = lax.rem(me, 2)
    base = me - core
    other = lax.rem(base + 2, peers)
    peer = (me, base + 1 - core, other + core, other + 1 - core)
    half_of = (core, 1 - core, core, 1 - core)

    loads = [pltpu.make_async_copy(x_ref.at[f], xpad.at[f, pl.ds(2, rows)], x_sem.at[f]) for f in range(nloc)]
    weights = [
        pltpu.make_async_copy(
            ref.at[dy, dx],
            wcat.at[which, pl.ds(dy * chans, chans), pl.ds(dx * chans, chans)],
            w_sem.at[which, 3 * dy + dx],
        )
        for which, ref in enumerate((w1_ref, w2_ref))
        for dy in range(3)
        for dx in range(3)
    ]
    edges = pltpu.make_async_copy(boundary_ref, bnd, b_sem)
    projections = [
        pltpu.make_async_copy(qkv_hbm, qkv_ref, p_sem.at[0]),
        pltpu.make_async_copy(outw_hbm, outw_ref, p_sem.at[1]),
    ]
    loads[0].start()
    for w in weights:
        w.start()
    for x in loads[1:]:
        x.start()
    for p in projections:
        p.start()
    edges.start()

    barrier = pltpu.get_barrier_semaphore()
    for k in range(1, 4):
        pl.semaphore_signal(barrier, inc=1, device_id={"tm": peer[k]}, device_id_type=MESH)

    @pl.when(place > 0)
    def _():
        pl.semaphore_signal(barrier, inc=1, device_id={"space": place - 1}, device_id_type=MESH)

    @pl.when(place < last)
    def _():
        pl.semaphore_signal(barrier, inc=1, device_id={"space": place + 1}, device_id_type=MESH)

    beside = jnp.where(place > 0, 1, 0) + jnp.where(place < last, 1, 0)
    pl.semaphore_wait(barrier, 3 + beside)

    def up(i):
        return pltpu.make_async_remote_copy(
            x_ref.at[:, i], xpad.at[:, rows + 2 + i], halo_send.at[0, i], halo_recv.at[0, i],
            device_id={"space": place - 1}, device_id_type=MESH,
        )

    def down(i):
        return pltpu.make_async_remote_copy(
            x_ref.at[:, rows - 1 - i], xpad.at[:, 1 - i], halo_send.at[1, i], halo_recv.at[1, i],
            device_id={"space": place + 1}, device_id_type=MESH,
        )

    @pl.when(place > 0)
    def _():
        up(0).start()
        up(1).start()

    @pl.when(place < last)
    def _():
        down(0).start()
        down(1).start()

    row_id = lax.broadcasted_iota(jnp.int32, mask_ref.shape, 0)
    col_id = lax.broadcasted_iota(jnp.int32, mask_ref.shape, 1)
    mask_ref[...] = jnp.where(lax.rem(row_id, GROUP) == lax.rem(col_id, GROUP), 0.0, -1e30)
    heads_of = lax.broadcasted_iota(jnp.int32, (2 * nloc * GROUP, chans), 1) // (chans // HEADS)
    gain = gain_ref[...]

    def strip(frame, side):
        scaled = (me * nloc + frame) * (coarse - 1)
        lower = scaled // (nframes - 1)
        upper = jnp.minimum(lower + 1, coarse - 1)
        frac = (scaled - lower * (nframes - 1)).astype(jnp.float32) / float(nframes - 1)
        low, high = bnd[lower, side].astype(jnp.float32), bnd[upper, side].astype(jnp.float32)
        return ((1.0 - frac) * low + frac * high).astype(jnp.bfloat16)

    def stacked(ref, frame, which):
        return jnp.concatenate([ref[frame, r].reshape(-1, chans) for r in which], axis=0)

    def hidden_rows(frame, which):
        taps = [stacked(xpad, frame, [r + dy for r in which]) for dy in range(3)]
        first = conv_taps(taps, wcat[0], width)
        act = (first / (1.0 + jnp.exp(-first))).astype(jnp.bfloat16)
        n = act.shape[0] // len(which)
        for i, r in enumerate(which):
            hpad[frame, r] = act[i * n : (i + 1) * n].reshape(n // width, width, chans)

    def resid_rows(frame, which, slot):
        taps = [stacked(hpad, frame, [r + dy for r in which]) for dy in range(3)]
        second = conv_taps(taps, wcat[1], width)
        before = stacked(xpad, frame, [r + 2 for r in which])
        resid = (before.astype(jnp.float32) + second).astype(jnp.bfloat16)
        wide = resid.astype(jnp.float32)
        mean_sq = jnp.mean(wide * wide, axis=-1, keepdims=True)
        normed = (wide * lax.rsqrt(mean_sq + 1e-06) * gain).astype(jnp.bfloat16)
        n = resid.shape[0] // len(which)
        for i in range(len(which)):
            rbuf[slot + i, frame] = resid[i * n : (i + 1) * n].reshape(n // width, width, chans)
            nbuf[slot + i, frame] = normed[i * n : (i + 1) * n].reshape(n // width, width, chans)

    def early(frame, k):
        to = 1 if k == 4 else k
        cols = pl.ds(pl.multiple_of(half_of[to] * half, half), half)
        src = (rbuf if k == 4 else nbuf).at[0, frame, cols]
        dst = rsib.at[0, frame] if k == 4 else nall.at[0, k - 1, frame]
        return pltpu.make_async_remote_copy(
            src, dst, early_send.at[frame, k - 1], early_recv.at[frame, k - 1],
            device_id={"tm": peer[to]}, device_id_type=MESH,
        )

    def there(slot, part, k):
        to = 1 if k == 4 else k
        begin = part * CELLS
        cols = pl.ds(pl.multiple_of(half_of[to] * half + begin, CELLS), CELLS)
        here = pl.ds(pl.multiple_of(begin, CELLS), CELLS)
        src = (rbuf if k == 4 else nbuf).at[slot, :, cols]
        dst = rsib.at[slot, :, here] if k == 4 else nall.at[slot, k - 1, :, here]
        return pltpu.make_async_remote_copy(
            src, dst, there_send.at[slot, part, k - 1], there_recv.at[slot, part, k - 1],
            device_id={"tm": peer[to]}, device_id_type=MESH,
        )

    order = (2, 3, 1, 4)
    parts = half // CELLS

    def send_slot(slot):
        for part in range(parts):
            for k in order:
                there(slot, part, k).start()

    for w in weights:
        w.wait()

    for x in loads[:BATCH]:
        x.wait()

    def first_pair(frame, carry):
        fr = pl.ds(frame * BATCH, BATCH)
        hidden_rows(fr, [2, 3, 4, 5])
        resid_rows(fr, [2, 3], 0)
        for i in range(BATCH):
            for k in order:
                early(frame * BATCH + i, k).start()
        return carry

    first_pair(0, 0)
    for x in loads[BATCH:]:
        x.wait()
    lax.fori_loop(1, nloc // BATCH, first_pair, 0)
    send_slot(1)

    def inner_pair(frame, carry):
        hidden_rows(pl.ds(0, nloc), [6, 7])
        resid_rows(pl.ds(0, nloc), [4, 5], 2)
        return carry

    inner_pair(0, 0)
    send_slot(2)
    send_slot(3)

    for p in projections:
        p.wait()
    edges.wait()

    def near_pair():
        @pl.when(place > 0)
        def _():
            down(0).wait_recv()

        @pl.when(place == 0)
        def _():
            for f in range(nloc):
                edge = strip(f, 0)
                xpad[f, 0] = edge
                xpad[f, 1] = edge

        @pl.when(place < last)
        def _():
            up(0).wait_recv()

        @pl.when(place == last)
        def _():
            for f in range(nloc):
                edge = strip(f, 1)
                xpad[f, rows + 2] = edge
                xpad[f, rows + 3] = edge

        def one(frame, carry):
            hidden_rows(pl.ds(0, nloc), [1, rows])
            resid_rows(pl.ds(0, nloc), [1, rows - 2], 4)
            return carry

        one(0, 0)
        send_slot(4)
        send_slot(5)

    def edge_pair():
        @pl.when(place > 0)
        def _():
            down(1).wait_recv()

        @pl.when(place < last)
        def _():
            up(1).wait_recv()

        def one(frame, carry):
            hidden_rows(pl.ds(0, nloc), [0, rows + 1])
            return carry

        one(0, 0)

        @pl.when(place == 0)
        def _():
            hpad[:, 0] = xpad[:, 1]

        @pl.when(place == last)
        def _():
            hpad[:, rows + 1] = xpad[:, rows + 2]

        def two(frame, carry):
            resid_rows(pl.ds(0, nloc), [0, rows - 1], 6)
            return carry

        two(0, 0)
        send_slot(6)
        send_slot(7)

    def row_of(slot):
        k = slot - 4
        far = lax.rem(k + 4, 2)
        outer = (1 - k // 2) * (1 - far) + (rows - 2 + k // 2) * far
        return jnp.where(slot < 4, slot + 2, outer)

    def back(slot, part):
        here = pl.ds(pl.multiple_of(part * CELLS, CELLS), CELLS)
        cols = pl.ds(pl.multiple_of(core * half + part * CELLS, CELLS), CELLS)
        return pltpu.make_async_remote_copy(
            abuf.at[slot, :, here], o_ref.at[:, row_of(slot), cols],
            back_send.at[slot, part], back_recv.at[slot, part],
            device_id={"tm": peer[1]}, device_id_type=MESH,
        )

    for f in range(nloc):
        for k in order:
            early(f, k).wait_recv()

    def step(s, carry):
        slot = s // parts
        part = lax.rem(s, parts)

        @pl.when(slot > 0)
        def _():
            for k in order:
                there(slot, part, k).wait_recv()

        here = pl.ds(pl.multiple_of(part * CELLS, CELLS), CELLS)
        cols = pl.ds(pl.multiple_of(core * half + part * CELLS, CELLS), CELLS)
        normed = jnp.concatenate(
            [nbuf[slot, :, cols, :], nall[slot, :, :, here, :].reshape(3 * nloc, CELLS, chans)], axis=0
        )
        resid = jnp.concatenate([rbuf[slot, :, cols, :], rsib[slot, :, here, :]], axis=0).astype(jnp.float32)
        out = attend(normed, resid, qkv_ref[...], outw_ref[...], mask_ref[...], heads_of).astype(jnp.bfloat16)
        abuf[slot, :, here, :] = out[nloc:]
        back(slot, part).start()
        o_ref[:, row_of(slot), cols, :] = out[:nloc]

        @pl.when(s == parts - 1)
        def _():
            near_pair()

        @pl.when(s == 3 * parts - 1)
        def _():
            edge_pair()

        return carry

    lax.fori_loop(0, rows * parts, step, 0)

    @pl.when(place > 0)
    def _():
        up(0).wait_send()
        up(1).wait_send()

    @pl.when(place < last)
    def _():
        down(0).wait_send()
        down(1).wait_send()

    for f in range(nloc):
        for k in order:
            early(f, k).wait_send()

    def drain(slot, carry):
        for part in range(parts):
            for k in order:
                there(slot, part, k).wait_send()
        return carry

    lax.fori_loop(1, rows, drain, 0)

    def settle(slot, carry):
        for part in range(parts):
            back(slot, part).wait()
        return carry

    lax.fori_loop(0, rows, settle, 0)


def on_device(frames_in, boundary, conv_first, conv_second, norm_gain, qkv_weight, out_weight):
    nloc, rows, width, chans = frames_in.shape
    peers = lax.axis_size("tm")
    spaces = lax.axis_size("space")
    nframes = nloc * peers
    half = width // 2
    parts = half // CELLS
    vmem = pl.BlockSpec(memory_space=pltpu.VMEM)
    hbm = pl.BlockSpec(memory_space=pl.ANY)
    bf16 = jnp.bfloat16
    dma = pltpu.SemaphoreType.DMA
    return pl.pallas_call(
        functools.partial(block_kernel, peers, spaces),
        out_shape=pltpu.VMEM(frames_in.shape, frames_in.dtype),
        in_specs=[hbm] * 4 + [vmem] + [hbm] * 2,
        out_specs=vmem,
        scratch_shapes=[
            pltpu.VMEM((nloc, rows + 4, width, chans), bf16),
            pltpu.VMEM((nloc, rows + 2, width, chans), bf16),
            pltpu.VMEM((rows, nloc, width, chans), bf16),
            pltpu.VMEM((rows, nloc, width, chans), bf16),
            pltpu.VMEM((rows, peers - 1, nloc, half, chans), bf16),
            pltpu.VMEM((rows, nloc, half, chans), bf16),
            pltpu.VMEM((rows, nloc, half, chans), bf16),
            pltpu.VMEM((2, 3 * chans, 3 * chans), bf16),
            pltpu.VMEM(boundary.shape, bf16),
            pltpu.VMEM(qkv_weight.shape, bf16),
            pltpu.VMEM(out_weight.shape, bf16),
            pltpu.VMEM((2 * nloc * GROUP, nframes * GROUP), jnp.float32),
            dma((nloc,)), dma((2, 9)), dma, dma((2,)), dma((2, 2)), dma((2, 2)),
            dma((nloc, 4)), dma((nloc, 4)), dma((rows, parts, 4)), dma((rows, parts, 4)),
            dma((rows, parts)), dma((rows, parts)),
        ],
        compiler_params=pltpu.CompilerParams(
            collective_id=0, has_side_effects=True, vmem_limit_bytes=54 * 1024 * 1024
        ),
        name="denoise",
    )(frames_in, boundary, conv_first, conv_second, norm_gain.reshape(1, chans), qkv_weight, out_weight)


def solution(mesh):
    placed = (P("tm", "space", None, None), P(), P(), P(), P(), P(), P())
    return jax.shard_map(
        on_device,
        mesh=mesh,
        in_specs=placed,
        out_specs=P("tm", "space", None, None),
        check_vma=False,
    )
```

```python
import functools

import jax
import jax.numpy as jnp
from jax import lax
from jax.experimental import pallas as pl
from jax.experimental.pallas import tpu as pltpu
from jax.sharding import PartitionSpec as P

HEADS = 8
MESH = pl.DeviceIdType.MESH
TILE = 8
TAIL = (32, 32)


def conv_taps(taps, weight, width):
    cells = jnp.concatenate(taps, axis=1)
    rows = cells.shape[0]
    chans = weight.shape[1] // 3
    wide = jnp.dot(cells, weight, preferred_element_type=jnp.float32)
    col = lax.rem(lax.broadcasted_iota(jnp.int32, (rows, chans), 0), width)
    left = jnp.where(col == 0, 0.0, pltpu.roll(wide[:, :chans], 1, 0))
    right = jnp.where(col == width - 1, 0.0, pltpu.roll(wide[:, 2 * chans :], rows - 1, 0))
    return wide[:, chans : 2 * chans] + left + right


def attend(normed, resid, qkv_weight, out_weight, mask, heads_of):
    nframes, cells, chans = normed.shape
    mine = resid.shape[0]
    head_dim = chans // HEADS
    keys = nframes * TILE
    asks = mine * TILE
    query = jnp.dot(
        normed[:mine].reshape(mine * cells, chans), qkv_weight[:, :chans], preferred_element_type=jnp.float32
    ).reshape(mine, cells, chans)
    kv = jnp.dot(
        normed.reshape(nframes * cells, chans), qkv_weight[:, chans:], preferred_element_type=jnp.float32
    ).reshape(nframes, cells, 2 * chans)
    outs, kept = [], []
    for j in range(0, cells, TILE):
        part = query[:, j : j + TILE].reshape(asks, chans).astype(jnp.bfloat16)
        part = part * jnp.bfloat16(1.0 / head_dim**0.5)
        pair = kv[:, j : j + TILE].reshape(keys, 2 * chans).astype(jnp.bfloat16)
        key_part, value = pair[:, :chans], pair[:, chans:]
        with_ones = jnp.concatenate([value, jnp.ones_like(value)], axis=1)
        picked = jnp.concatenate(
            [jnp.where(heads_of == h, part, jnp.zeros_like(part)) for h in range(HEADS)], axis=0
        )
        scores = lax.dot_general(
            picked, key_part, (((1,), (1,)), ((), ())), preferred_element_type=jnp.float32
        )
        scores = (scores.reshape(HEADS, asks, keys) + mask).reshape(HEADS * asks, keys)
        top = jnp.max(scores, axis=-1, keepdims=True)
        expd = jnp.exp((scores - top).astype(jnp.bfloat16))
        both = jnp.dot(expd, with_ones, preferred_element_type=jnp.float32)
        num, den = both[:asks, :chans], both[:asks, chans:]
        for h in range(1, HEADS):
            piece = both[h * asks : (h + 1) * asks]
            own = heads_of == h
            num = jnp.where(own, piece[:, :chans], num)
            den = jnp.where(own, piece[:, chans:], den)
        outs.append((num / den).astype(jnp.bfloat16))
        kept.append(resid[:, j : j + TILE].reshape(asks, chans))
    attended = jnp.concatenate(outs, axis=0)
    out = jnp.concatenate(kept, axis=0) + jnp.dot(attended, out_weight, preferred_element_type=jnp.float32)
    parts = [out[g * asks : (g + 1) * asks].reshape(mine, TILE, chans) for g in range(cells // TILE)]
    return jnp.concatenate(parts, axis=1)


def block_kernel(
    peers, spaces,
    x_ref, boundary_ref, w1_ref, w2_ref, gain_hbm, qkv_hbm, outw_hbm, o_ref,
    xpad, hpad, rbuf, nbuf, nall, rsib, abuf, wcat, bnd, gain_ref, qkv_ref, outw_ref, mask_ref,
    x_sem, w_sem, b_sem, p_sem, halo_send, halo_recv, there_send, there_recv, back_send, back_recv, own_sem,
):
    nloc, rows, width, chans = x_ref.shape
    coarse = boundary_ref.shape[0]
    nframes = nloc * peers
    half = width // 2
    me = lax.axis_index("tm")
    place = lax.axis_index("space")
    last = spaces - 1
    core = lax.rem(me, 2)
    sibling = me + 1 - 2 * core
    across = lax.rem(me + 2, peers)
    crossed = lax.rem(sibling + 2, peers)

    def load(f):
        return pltpu.make_async_copy(x_ref.at[f], xpad.at[f, pl.ds(2, rows)], x_sem.at[f])

    weights = [
        [
            pltpu.make_async_copy(
                ref.at[dy, dx],
                wcat.at[which, pl.ds(dy * chans, chans), pl.ds(dx * chans, chans)],
                w_sem.at[which, 3 * dy + dx],
            )
            for dy in range(3)
            for dx in range(3)
        ]
        for which, ref in enumerate((w1_ref, w2_ref))
    ]
    edges = pltpu.make_async_copy(boundary_ref, bnd, b_sem)
    gains = pltpu.make_async_copy(gain_hbm, gain_ref, p_sem.at[2])
    projections = [
        pltpu.make_async_copy(qkv_hbm, qkv_ref, p_sem.at[0]),
        pltpu.make_async_copy(outw_hbm, outw_ref, p_sem.at[1]),
    ]
    for c in [load(0)] + weights[0] + weights[1] + [gains] + [load(f) for f in range(1, nloc)] + projections + [edges]:
        c.start()

    barrier = pltpu.get_barrier_semaphore()
    for k in (sibling, across, crossed):
        pl.semaphore_signal(barrier, inc=1, device_id={"tm": k}, device_id_type=MESH)

    @pl.when(place > 0)
    def _():
        pl.semaphore_signal(barrier, inc=1, device_id={"space": place - 1}, device_id_type=MESH)

    @pl.when(place < last)
    def _():
        pl.semaphore_signal(barrier, inc=1, device_id={"space": place + 1}, device_id_type=MESH)

    beside = jnp.where(place > 0, 1, 0) + jnp.where(place < last, 1, 0)
    pl.semaphore_wait(barrier, 3 + beside)

    def up(i):
        return pltpu.make_async_remote_copy(
            x_ref.at[:, i], xpad.at[:, rows + 2 + i], halo_send.at[0, i], halo_recv.at[0, i],
            device_id={"space": place - 1}, device_id_type=MESH,
        )

    def down(i):
        return pltpu.make_async_remote_copy(
            x_ref.at[:, rows - 1 - i], xpad.at[:, 1 - i], halo_send.at[1, i], halo_recv.at[1, i],
            device_id={"space": place + 1}, device_id_type=MESH,
        )

    @pl.when(place > 0)
    def _():
        up(0).start()
        up(1).start()

    @pl.when(place < last)
    def _():
        down(0).start()
        down(1).start()

    row_id = lax.broadcasted_iota(jnp.int32, mask_ref.shape, 0)
    col_id = lax.broadcasted_iota(jnp.int32, mask_ref.shape, 1)
    mask_ref[...] = jnp.where(lax.rem(row_id, TILE) == lax.rem(col_id, TILE), 0.0, -1e30)
    heads_of = lax.broadcasted_iota(jnp.int32, (2 * nloc * TILE, chans), 1) // (chans // HEADS)

    def strip(frame, side):
        scaled = (me * nloc + frame) * (coarse - 1)
        lower = scaled // (nframes - 1)
        upper = jnp.minimum(lower + 1, coarse - 1)
        frac = (scaled - lower * (nframes - 1)).astype(jnp.float32) / float(nframes - 1)
        low, high = bnd[lower, side].astype(jnp.float32), bnd[upper, side].astype(jnp.float32)
        return ((1.0 - frac) * low + frac * high).astype(jnp.bfloat16)

    def stacked(ref, frames, which):
        return jnp.concatenate([ref[frames, r].reshape(-1, chans) for r in which], axis=0)

    def hidden_rows(frames, which):
        taps = [stacked(xpad, frames, [r + dy for r in which]) for dy in range(3)]
        first = conv_taps(taps, wcat[0], width)
        act = (first / (1.0 + jnp.exp(-first))).astype(jnp.bfloat16)
        n = act.shape[0] // len(which)
        for i, r in enumerate(which):
            hpad[frames, r] = act[i * n : (i + 1) * n].reshape(n // width, width, chans)

    def resid_rows(frames, which, slot):
        taps = [stacked(hpad, frames, [r + dy for r in which]) for dy in range(3)]
        second = conv_taps(taps, wcat[1], width)
        before = stacked(xpad, frames, [r + 2 for r in which])
        resid = (before.astype(jnp.float32) + second).astype(jnp.bfloat16)
        wide = resid.astype(jnp.float32)
        mean_sq = jnp.mean(wide * wide, axis=-1, keepdims=True)
        normed = (wide * lax.rsqrt(mean_sq + 1e-06) * gain_ref[...]).astype(jnp.bfloat16)
        n = wide.shape[0] // len(which)
        for i in range(len(which)):
            for ref, v in ((rbuf, resid), (nbuf, normed)):
                v = v[i * n : (i + 1) * n].reshape(n // width, width, chans)
                ref[slot + i, 0, frames] = v[:, :half]
                ref[slot + i, 1, frames] = v[:, half:]

    def piece(slot, frames, begin, size, unit, k):
        side = core if k == 2 else 1 - core
        here = pl.ds(begin, size)
        src = (rbuf if k == 1 else nbuf).at[slot, side, frames, here]
        dst = rsib.at[slot, frames, here] if k == 1 else nall.at[slot, max(k - 1, 0), frames, here]
        return pltpu.make_async_remote_copy(
            src, dst, there_send.at[unit, k], there_recv.at[unit, k],
            device_id={"tm": sibling if k < 2 else crossed if k == 3 else across}, device_id_type=MESH,
        )

    every = pl.ds(0, nloc)
    batches = [pl.ds(0, 1), pl.ds(1, 2), pl.ds(3, nloc - 3)]
    early = [functools.partial(piece, 0, frames, 0, half, i) for i, frames in enumerate(batches)]

    def whole(slot):
        return functools.partial(piece, slot, every, 0, half, len(early) + slot - 1)

    starts = [sum(TAIL[:i]) for i in range(len(TAIL))]
    late = [
        functools.partial(piece, rows - 1, every, at, size, len(early) + rows - 2 + i)
        for i, (at, size) in enumerate(zip(starts, TAIL))
    ]

    def send(unit):
        for k in (2, 3, 0, 1):
            unit(k).start()

    for c in weights[0]:
        c.wait()
    for i, frames in enumerate(batches):
        for f in range(frames.start, frames.start + frames.size):
            load(f).wait()
        hidden_rows(frames, [2, 3, 4])
        if i == 0:
            for c in weights[1] + [gains]:
                c.wait()
        resid_rows(frames, [2], 0)
        for k in (2, 3, 0, 1):
            early[i](k).start()
    hidden_rows(every, [5])
    resid_rows(every, [3], 1)
    send(whole(1))
    hidden_rows(every, [6, 7])
    resid_rows(every, [4, 5], 2)
    send(whole(2))
    send(whole(3))

    for c in projections + [edges]:
        c.wait()

    def near_pair():
        @pl.when(place > 0)
        def _():
            down(0).wait_recv()

        @pl.when(place == 0)
        def _():
            for f in range(nloc):
                edge = strip(f, 0)
                xpad[f, 0] = edge
                xpad[f, 1] = edge

        @pl.when(place < last)
        def _():
            up(0).wait_recv()

        @pl.when(place == last)
        def _():
            for f in range(nloc):
                edge = strip(f, 1)
                xpad[f, rows + 2] = edge
                xpad[f, rows + 3] = edge

        hidden_rows(every, [1, rows])
        resid_rows(every, [1, rows - 2], 4)
        send(whole(4))
        send(whole(5))

    def edge_pair():

        @pl.when(place > 0)
        def _():
            down(1).wait_recv()

        @pl.when(place < last)
        def _():
            up(1).wait_recv()

        hidden_rows(every, [0, rows + 1])

        @pl.when(place == 0)
        def _():
            hpad[:, 0] = xpad[:, 1]

        @pl.when(place == last)
        def _():
            hpad[:, rows + 1] = xpad[:, rows + 2]

        resid_rows(every, [0, rows - 1], 6)
        send(whole(6))
        for unit in late:
            send(unit)

    def row_of(slot):
        k = slot - 4
        far = lax.rem(k + 4, 2)
        outer = (1 - k // 2) * (1 - far) + (rows - 2 + k // 2) * far
        return jnp.where(slot < 4, slot + 2, outer)

    def results(slot, row, begin, size, unit):
        here = pl.ds(begin, size)
        cols = pl.ds(pl.multiple_of(core * half + begin, size), size)
        mine = pltpu.make_async_copy(abuf.at[slot, pl.ds(0, nloc), here], o_ref.at[:, row, cols], own_sem.at[unit])
        theirs = pltpu.make_async_remote_copy(
            abuf.at[slot, pl.ds(nloc, nloc), here], o_ref.at[:, row, cols],
            back_send.at[unit], back_recv.at[unit], device_id={"tm": sibling}, device_id_type=MESH,
        )
        return mine, theirs

    def consume(slot, row, begin, size, unit):
        here = pl.ds(begin, size)
        normed = jnp.concatenate(
            [nbuf[slot, core, :, here, :], nall[slot, :, :, here, :].reshape(3 * nloc, size, chans)], axis=0
        )
        resid = jnp.concatenate([rbuf[slot, core, :, here, :], rsib[slot, :, here, :]], axis=0).astype(jnp.float32)
        out = attend(normed, resid, qkv_ref[...], outw_ref[...], mask_ref[...], heads_of)
        abuf[slot, :, here, :] = out.astype(jnp.bfloat16)
        mine, theirs = results(slot, row, begin, size, unit)
        theirs.start()
        mine.start()

    for unit in early:
        for k in range(4):
            unit(k).wait_recv()

    def step(slot, carry):
        @pl.when(slot > 0)
        def _():
            for k in range(4):
                whole(slot)(k).wait_recv()

        consume(slot, row_of(slot), 0, half, slot)

        @pl.when(slot == 1)
        def _():
            near_pair()

        @pl.when(slot == 3)
        def _():
            edge_pair()

        return carry

    lax.fori_loop(0, rows - 1, step, 0)
    for i, unit in enumerate(late):
        for k in range(4):
            unit(k).wait_recv()
        consume(rows - 1, rows - 1, starts[i], TAIL[i], rows - 1 + i)

    @pl.when(place > 0)
    def _():
        up(0).wait_send()
        up(1).wait_send()

    @pl.when(place < last)
    def _():
        down(0).wait_send()
        down(1).wait_send()

    for unit in early + late:
        for k in range(4):
            unit(k).wait_send()

    def drain(slot, carry):
        for k in range(4):
            whole(slot)(k).wait_send()
        return carry

    lax.fori_loop(1, rows - 1, drain, 0)

    def settle(slot, carry):
        for c in results(slot, row_of(slot), 0, half, slot):
            c.wait()
        return carry

    lax.fori_loop(0, rows - 1, settle, 0)
    for i in range(len(TAIL)):
        for c in results(rows - 1, rows - 1, starts[i], TAIL[i], rows - 1 + i):
            c.wait()


def on_device(frames_in, boundary, conv_first, conv_second, norm_gain, qkv_weight, out_weight):
    nloc, rows, width, chans = frames_in.shape
    peers = lax.axis_size("tm")
    spaces = lax.axis_size("space")
    nframes = nloc * peers
    half = width // 2
    units = 3 + rows - 2 + len(TAIL)
    hbm = pl.BlockSpec(memory_space=pl.ANY)
    bf16 = jnp.bfloat16
    dma = pltpu.SemaphoreType.DMA
    return pl.pallas_call(
        functools.partial(block_kernel, peers, spaces),
        out_shape=pltpu.VMEM(frames_in.shape, frames_in.dtype),
        in_specs=[hbm] * 7,
        out_specs=hbm,
        scratch_shapes=[
            pltpu.VMEM((nloc, rows + 4, width, chans), bf16),
            pltpu.VMEM((nloc, rows + 2, width, chans), bf16),
            pltpu.VMEM((rows, 2, nloc, half, chans), bf16),
            pltpu.VMEM((rows, 2, nloc, half, chans), bf16),
            pltpu.VMEM((rows, peers - 1, nloc, half, chans), bf16),
            pltpu.VMEM((rows, nloc, half, chans), bf16),
            pltpu.VMEM((rows, 2 * nloc, half, chans), bf16),
            pltpu.VMEM((2, 3 * chans, 3 * chans), bf16),
            pltpu.VMEM(boundary.shape, bf16),
            pltpu.VMEM((1, chans), jnp.float32),
            pltpu.VMEM(qkv_weight.shape, bf16),
            pltpu.VMEM(out_weight.shape, bf16),
            pltpu.VMEM((2 * nloc * TILE, nframes * TILE), jnp.float32),
            dma((nloc,)), dma((2, 9)), dma, dma((3,)), dma((2, 2)), dma((2, 2)),
            dma((units, 4)), dma((units, 4)),
            dma((rows - 1 + len(TAIL),)), dma((rows - 1 + len(TAIL),)), dma((rows - 1 + len(TAIL),)),
        ],
        compiler_params=pltpu.CompilerParams(
            collective_id=0, has_side_effects=True, vmem_limit_bytes=54 * 1024 * 1024
        ),
        name="denoise",
    )(frames_in, boundary, conv_first, conv_second, norm_gain.reshape(1, chans), qkv_weight, out_weight)


def solution(mesh):
    placed = (P("tm", "space", None, None), P(), P(), P(), P(), P(), P())
    return jax.shard_map(
        on_device,
        mesh=mesh,
        in_specs=placed,
        out_specs=P("tm", "space", None, None),
        check_vma=False,
    )
```

```python
import functools

import jax
import jax.numpy as jnp
from jax import lax
from jax.experimental import pallas as pl
from jax.experimental.pallas import tpu as pltpu
from jax.sharding import PartitionSpec as P

HEADS = 8
MESH = pl.DeviceIdType.MESH
TILE = 8
TAIL = (32, 32)


def conv_taps(taps, weight, width):
    cells = jnp.concatenate(taps, axis=1)
    rows = cells.shape[0]
    chans = weight.shape[1] // 3
    wide = jnp.dot(cells, weight, preferred_element_type=jnp.float32)
    col = lax.rem(lax.broadcasted_iota(jnp.int32, (rows, chans), 0), width)
    left = jnp.where(col == 0, 0.0, pltpu.roll(wide[:, :chans], 1, 0))
    right = jnp.where(col == width - 1, 0.0, pltpu.roll(wide[:, 2 * chans :], rows - 1, 0))
    return wide[:, chans : 2 * chans] + left + right


def attend(normed, resid, qkv_weight, out_weight, mask):
    nframes, cells, chans = normed.shape
    mine = resid.shape[0]
    head_dim = chans // HEADS
    keys = nframes * TILE
    asks = mine * TILE
    query = jnp.dot(
        normed[:mine].reshape(mine * cells, chans), qkv_weight[:, :chans], preferred_element_type=jnp.float32
    ).reshape(mine, cells, chans)
    kv = jnp.dot(
        normed.reshape(nframes * cells, chans), qkv_weight[:, chans:], preferred_element_type=jnp.float32
    ).reshape(nframes, cells, 2 * chans)
    heads_of = lax.broadcasted_iota(jnp.int32, (asks, chans), 1) // head_dim
    mask = mask[:asks]
    outs, kept = [], []
    for j in range(0, cells, TILE):
        part = query[:, j : j + TILE].reshape(asks, chans).astype(jnp.bfloat16)
        part = part * jnp.bfloat16(1.0 / head_dim**0.5)
        pair = kv[:, j : j + TILE].reshape(keys, 2 * chans).astype(jnp.bfloat16)
        key_part, value = pair[:, :chans], pair[:, chans:]
        with_ones = jnp.concatenate([value, jnp.ones_like(value)], axis=1)
        picked = jnp.concatenate(
            [jnp.where(heads_of == h, part, jnp.zeros_like(part)) for h in range(HEADS)], axis=0
        )
        scores = lax.dot_general(
            picked, key_part, (((1,), (1,)), ((), ())), preferred_element_type=jnp.float32
        )
        scores = (scores.reshape(HEADS, asks, keys) + mask).reshape(HEADS * asks, keys)
        top = jnp.max(scores, axis=-1, keepdims=True)
        expd = jnp.exp((scores - top).astype(jnp.bfloat16))
        both = jnp.dot(expd, with_ones, preferred_element_type=jnp.float32)
        num, den = both[:asks, :chans], both[:asks, chans:]
        for h in range(1, HEADS):
            piece = both[h * asks : (h + 1) * asks]
            own = heads_of == h
            num = jnp.where(own, piece[:, :chans], num)
            den = jnp.where(own, piece[:, chans:], den)
        outs.append((num / den).astype(jnp.bfloat16))
        kept.append(resid[:, j : j + TILE].reshape(asks, chans))
    attended = jnp.concatenate(outs, axis=0)
    out = jnp.concatenate(kept, axis=0) + jnp.dot(attended, out_weight, preferred_element_type=jnp.float32)
    parts = [out[g * asks : (g + 1) * asks].reshape(mine, TILE, chans) for g in range(cells // TILE)]
    return jnp.concatenate(parts, axis=1)


def block_kernel(
    peers, spaces,
    x_ref, boundary_ref, w1_ref, w2_ref, gain_hbm, qkv_hbm, outw_hbm, o_ref,
    xpad, hpad, rbuf, nbuf, nall, rsib, abuf, taps_ref, quad, qbuf, bnd, gain_ref, qkv_ref, outw_ref, mask_ref,
    x_sem, w_sem, b_sem, p_sem, halo_send, halo_recv, there_send, there_recv, back_send, back_recv, own_sem, share_send, share_recv,
):
    nloc, rows, width, chans = x_ref.shape
    coarse = boundary_ref.shape[0]
    nframes = nloc * peers
    half = width // 2
    me = lax.axis_index("tm")
    place = lax.axis_index("space")
    last = spaces - 1
    core = lax.rem(me, 2)
    sibling = me + 1 - 2 * core
    across = lax.rem(me + 2, peers)
    crossed = lax.rem(sibling + 2, peers)

    batches = [pl.ds(0, 1), pl.ds(1, 2), pl.ds(3, nloc - 3)]

    def load(i):
        frames = batches[i]
        return pltpu.make_async_copy(x_ref.at[frames], xpad.at[frames, pl.ds(2, rows)], x_sem.at[i])

    weights = [
        pltpu.make_async_copy(ref, taps_ref.at[which], w_sem.at[which]) for which, ref in enumerate((w1_ref, w2_ref))
    ]
    edges = pltpu.make_async_copy(boundary_ref, bnd, b_sem)
    gains = pltpu.make_async_copy(gain_hbm, gain_ref, p_sem.at[2])
    projections = [
        pltpu.make_async_copy(qkv_hbm, qkv_ref, p_sem.at[0]),
        pltpu.make_async_copy(outw_hbm, outw_ref, p_sem.at[1]),
    ]
    for c in [load(0)] + weights + [gains, load(1), load(2)] + projections + [edges]:
        c.start()

    barrier = pltpu.get_barrier_semaphore()
    for k in (sibling, across, crossed):
        pl.semaphore_signal(barrier, inc=1, device_id={"tm": k}, device_id_type=MESH)

    @pl.when(place > 0)
    def _():
        pl.semaphore_signal(barrier, inc=1, device_id={"space": place - 1}, device_id_type=MESH)

    @pl.when(place < last)
    def _():
        pl.semaphore_signal(barrier, inc=1, device_id={"space": place + 1}, device_id_type=MESH)

    beside = jnp.where(place > 0, 1, 0) + jnp.where(place < last, 1, 0)
    pl.semaphore_wait(barrier, 3 + beside)

    def up(i):
        return pltpu.make_async_remote_copy(
            x_ref.at[:, i], xpad.at[:, rows + 2 + i], halo_send.at[0, i], halo_recv.at[0, i],
            device_id={"space": place - 1}, device_id_type=MESH,
        )

    def down(i):
        return pltpu.make_async_remote_copy(
            x_ref.at[:, rows - 1 - i], xpad.at[:, 1 - i], halo_send.at[1, i], halo_recv.at[1, i],
            device_id={"space": place + 1}, device_id_type=MESH,
        )

    @pl.when(place > 0)
    def _():
        up(0).start()
        up(1).start()

    @pl.when(place < last)
    def _():
        down(0).start()
        down(1).start()

    row_id = lax.broadcasted_iota(jnp.int32, mask_ref.shape, 0)
    col_id = lax.broadcasted_iota(jnp.int32, mask_ref.shape, 1)
    mask_ref[...] = jnp.where(lax.rem(row_id, TILE) == lax.rem(col_id, TILE), 0.0, -1e30)
    def strip(frame, side):
        scaled = (me * nloc + frame) * (coarse - 1)
        lower = scaled // (nframes - 1)
        upper = jnp.minimum(lower + 1, coarse - 1)
        frac = (scaled - lower * (nframes - 1)).astype(jnp.float32) / float(nframes - 1)
        low, high = bnd[lower, side].astype(jnp.float32), bnd[upper, side].astype(jnp.float32)
        return ((1.0 - frac) * low + frac * high).astype(jnp.bfloat16)

    def kernel_of(which):
        return jnp.concatenate(
            [jnp.concatenate([taps_ref[which, dy, dx] for dx in range(3)], axis=1) for dy in range(3)], axis=0
        )

    def stacked(ref, frames, which):
        return jnp.concatenate([ref[frames, r].reshape(-1, chans) for r in which], axis=0)

    def hidden_rows(frames, which):
        taps = [stacked(xpad, frames, [r + dy for r in which]) for dy in range(3)]
        first = conv_taps(taps, kernel_of(0), width)
        act = (first / (1.0 + jnp.exp(-first))).astype(jnp.bfloat16)
        n = act.shape[0] // len(which)
        for i, r in enumerate(which):
            hpad[frames, r] = act[i * n : (i + 1) * n].reshape(n // width, width, chans)

    def resid_rows(frames, which, slot):
        taps = [stacked(hpad, frames, [r + dy for r in which]) for dy in range(3)]
        second = conv_taps(taps, kernel_of(1), width)
        before = stacked(xpad, frames, [r + 2 for r in which])
        resid = (before.astype(jnp.float32) + second).astype(jnp.bfloat16)
        wide = resid.astype(jnp.float32)
        normed = norm(wide)
        n = wide.shape[0] // len(which)
        for i in range(len(which)):
            for ref, v in ((rbuf, resid), (nbuf, normed)):
                v = v[i * n : (i + 1) * n].reshape(n // width, width, chans)
                ref[slot + i, 0, frames] = v[:, :half]
                ref[slot + i, 1, frames] = v[:, half:]

    def piece(slot, frames, begin, size, unit, k):
        side = core if k == 2 else 1 - core
        here = pl.ds(begin, size)
        src = (rbuf if k == 1 else nbuf).at[slot, side, frames, here]
        dst = rsib.at[slot, frames, here] if k == 1 else nall.at[slot, max(k - 1, 0), frames, here]
        return pltpu.make_async_remote_copy(
            src, dst, there_send.at[unit, k], there_recv.at[unit, k],
            device_id={"tm": sibling if k < 2 else crossed if k == 3 else across}, device_id_type=MESH,
        )

    every = pl.ds(0, nloc)
    early = [functools.partial(piece, 0, frames, 0, half, i) for i, frames in enumerate(batches)]

    def whole(slot):
        return functools.partial(piece, slot, every, 0, half, len(early) + slot - 1)

    starts = [sum(TAIL[:i]) for i in range(len(TAIL))]
    late = [
        functools.partial(piece, rows - 2, every, at, size, len(early) + rows - 3 + i)
        for i, (at, size) in enumerate(zip(starts, TAIL))
    ]

    group = (me, sibling, across, crossed)
    quarter = width // peers

    def share(k):
        to = group[k]
        begin = pl.multiple_of(lax.rem(to, 2) * quarter, quarter)
        return pltpu.make_async_remote_copy(
            rbuf.at[rows - 1, to // 2, :, pl.ds(begin, quarter)], quad.at[k - 1],
            share_send.at[0, k - 1], share_recv.at[0, k - 1], device_id={"tm": to}, device_id_type=MESH,
        )

    def reply(k):
        cols = pl.ds(pl.multiple_of(me * quarter, quarter), quarter)
        dst = o_ref.at[:, rows - 1, cols]
        if k == 0:
            return pltpu.make_async_copy(qbuf.at[0], dst, own_sem.at[rows - 2 + len(TAIL)])
        return pltpu.make_async_remote_copy(
            qbuf.at[k], dst, share_send.at[1, k - 1], share_recv.at[1, k - 1],
            device_id={"tm": group[k]}, device_id_type=MESH,
        )

    def norm(wide):
        mean_sq = jnp.mean(wide * wide, axis=-1, keepdims=True)
        return (wide * lax.rsqrt(mean_sq + 1e-06) * gain_ref[...]).astype(jnp.bfloat16)

    def send(unit):
        for k in (2, 3, 0, 1):
            unit(k).start()

    weights[0].wait()
    for i, frames in enumerate(batches):
        load(i).wait()
        hidden_rows(frames, [2, 3, 4])
        if i == 0:
            weights[1].wait()
            gains.wait()
        resid_rows(frames, [2], 0)
        for k in (2, 3, 0, 1):
            early[i](k).start()
    hidden_rows(every, [5])
    resid_rows(every, [3], 1)
    send(whole(1))
    hidden_rows(every, [6, 7])
    resid_rows(every, [4, 5], 2)
    send(whole(2))
    send(whole(3))

    for c in projections + [edges]:
        c.wait()

    def near_pair():
        @pl.when(place > 0)
        def _():
            down(0).wait_recv()

        @pl.when(place == 0)
        def _():
            for f in range(nloc):
                edge = strip(f, 0)
                xpad[f, 0] = edge
                xpad[f, 1] = edge

        @pl.when(place < last)
        def _():
            up(0).wait_recv()

        @pl.when(place == last)
        def _():
            for f in range(nloc):
                edge = strip(f, 1)
                xpad[f, rows + 2] = edge
                xpad[f, rows + 3] = edge

        hidden_rows(every, [1, rows])
        resid_rows(every, [1, rows - 2], 4)
        send(whole(4))
        send(whole(5))

    def edge_pair():

        @pl.when(place > 0)
        def _():
            down(1).wait_recv()

        @pl.when(place < last)
        def _():
            up(1).wait_recv()

        hidden_rows(every, [0, rows + 1])

        @pl.when(place == 0)
        def _():
            hpad[:, 0] = xpad[:, 1]

        @pl.when(place == last)
        def _():
            hpad[:, rows + 1] = xpad[:, rows + 2]

        resid_rows(every, [0, rows - 1], 6)
        for k in (2, 3, 1):
            share(k).start()
        for unit in late:
            send(unit)

    def row_of(slot):
        k = slot - 4
        far = lax.rem(k + 4, 2)
        outer = (1 - k // 2) * (1 - far) + (rows - 2 + k // 2) * far
        return jnp.where(slot < 4, slot + 2, outer)

    def results(slot, row, begin, size, unit):
        here = pl.ds(begin, size)
        cols = pl.ds(pl.multiple_of(core * half + begin, size), size)
        mine = pltpu.make_async_copy(abuf.at[slot, pl.ds(0, nloc), here], o_ref.at[:, row, cols], own_sem.at[unit])
        theirs = pltpu.make_async_remote_copy(
            abuf.at[slot, pl.ds(nloc, nloc), here], o_ref.at[:, row, cols],
            back_send.at[unit], back_recv.at[unit], device_id={"tm": sibling}, device_id_type=MESH,
        )
        return mine, theirs

    def consume(slot, row, begin, size, unit):
        here = pl.ds(begin, size)
        normed = jnp.concatenate(
            [nbuf[slot, core, :, here, :], nall[slot, :, :, here, :].reshape(3 * nloc, size, chans)], axis=0
        )
        resid = jnp.concatenate([rbuf[slot, core, :, here, :], rsib[slot, :, here, :]], axis=0).astype(jnp.float32)
        out = attend(normed, resid, qkv_ref[...], outw_ref[...], mask_ref[...])
        abuf[slot, :, here, :] = out.astype(jnp.bfloat16)
        mine, theirs = results(slot, row, begin, size, unit)
        theirs.start()
        mine.start()

    for unit in early:
        for k in range(4):
            unit(k).wait_recv()

    def step(slot, carry):
        @pl.when(slot > 0)
        def _():
            for k in range(4):
                whole(slot)(k).wait_recv()

        consume(slot, row_of(slot), 0, half, slot)

        @pl.when(slot == 1)
        def _():
            near_pair()

        @pl.when(slot == 3)
        def _():
            edge_pair()

        return carry

    lax.fori_loop(0, rows - 2, step, 0)

    for k in (1, 2, 3):
        share(k).wait_recv()
    begin = pl.multiple_of(core * quarter, quarter)
    mine = rbuf[rows - 1, me // 2, :, pl.ds(begin, quarter), :]
    resid = jnp.concatenate([mine, quad[...].reshape(3 * nloc, quarter, chans)], axis=0).astype(jnp.float32)
    normed = norm(resid.reshape(nframes * quarter, chans)).reshape(nframes, quarter, chans)
    out = attend(normed, resid, qkv_ref[...], outw_ref[...], mask_ref[...])
    qbuf[...] = out.astype(jnp.bfloat16).reshape(peers, nloc, quarter, chans)
    for k in (2, 3, 1, 0):
        reply(k).start()

    for i, unit in enumerate(late):
        for k in range(4):
            unit(k).wait_recv()
        consume(rows - 2, 0, starts[i], TAIL[i], rows - 2 + i)

    @pl.when(place > 0)
    def _():
        up(0).wait_send()
        up(1).wait_send()

    @pl.when(place < last)
    def _():
        down(0).wait_send()
        down(1).wait_send()

    for unit in early + late:
        for k in range(4):
            unit(k).wait_send()

    def drain(slot, carry):
        for k in range(4):
            whole(slot)(k).wait_send()
        return carry

    lax.fori_loop(1, rows - 2, drain, 0)
    for k in (1, 2, 3):
        share(k).wait_send()
        reply(k).wait()
    reply(0).wait()

    def settle(slot, carry):
        for c in results(slot, row_of(slot), 0, half, slot):
            c.wait()
        return carry

    lax.fori_loop(0, rows - 2, settle, 0)
    for i in range(len(TAIL)):
        for c in results(rows - 2, 0, starts[i], TAIL[i], rows - 2 + i):
            c.wait()


def on_device(frames_in, boundary, conv_first, conv_second, norm_gain, qkv_weight, out_weight):
    nloc, rows, width, chans = frames_in.shape
    peers = lax.axis_size("tm")
    spaces = lax.axis_size("space")
    nframes = nloc * peers
    half = width // 2
    units = 3 + rows - 3 + len(TAIL)
    hbm = pl.BlockSpec(memory_space=pl.ANY)
    bf16 = jnp.bfloat16
    dma = pltpu.SemaphoreType.DMA
    return pl.pallas_call(
        functools.partial(block_kernel, peers, spaces),
        out_shape=pltpu.VMEM(frames_in.shape, frames_in.dtype),
        in_specs=[hbm] * 7,
        out_specs=hbm,
        scratch_shapes=[
            pltpu.VMEM((nloc, rows + 4, width, chans), bf16),
            pltpu.VMEM((nloc, rows + 2, width, chans), bf16),
            pltpu.VMEM((rows, 2, nloc, half, chans), bf16),
            pltpu.VMEM((rows, 2, nloc, half, chans), bf16),
            pltpu.VMEM((rows, peers - 1, nloc, half, chans), bf16),
            pltpu.VMEM((rows, nloc, half, chans), bf16),
            pltpu.VMEM((rows, 2 * nloc, half, chans), bf16),
            pltpu.VMEM((2, *conv_first.shape), bf16),
            pltpu.VMEM((peers - 1, nloc, width // peers, chans), bf16),
            pltpu.VMEM((peers, nloc, width // peers, chans), bf16),
            pltpu.VMEM(boundary.shape, bf16),
            pltpu.VMEM((1, chans), jnp.float32),
            pltpu.VMEM(qkv_weight.shape, bf16),
            pltpu.VMEM(out_weight.shape, bf16),
            pltpu.VMEM((nframes * TILE, nframes * TILE), jnp.float32),
            dma((3,)), dma((2,)), dma, dma((3,)), dma((2, 2)), dma((2, 2)),
            dma((units, 4)), dma((units, 4)),
            dma((rows - 2 + len(TAIL),)), dma((rows - 2 + len(TAIL),)), dma((rows - 1 + len(TAIL),)),
            dma((2, 3)), dma((2, 3)),
        ],
        compiler_params=pltpu.CompilerParams(
            collective_id=0, has_side_effects=True, vmem_limit_bytes=54 * 1024 * 1024
        ),
        name="denoise",
    )(frames_in, boundary, conv_first, conv_second, norm_gain.reshape(1, chans), qkv_weight, out_weight)


def solution(mesh):
    placed = (P("tm", "space", None, None), P(), P(), P(), P(), P(), P())
    return jax.shard_map(
        on_device,
        mesh=mesh,
        in_specs=placed,
        out_specs=P("tm", "space", None, None),
        check_vma=False,
    )
```

```python
import functools

import jax
import jax.numpy as jnp
from jax import lax
from jax.experimental import pallas as pl
from jax.experimental.pallas import tpu as pltpu
from jax.sharding import PartitionSpec as P

HEADS = 8
MESH = pl.DeviceIdType.MESH
TILE = 8
TAIL = (32, 32)
SHARED = 1


def conv_taps(taps, weight, width):
    cells = jnp.concatenate(taps, axis=1)
    rows = cells.shape[0]
    chans = weight.shape[1] // 3
    wide = jnp.dot(cells, weight, preferred_element_type=jnp.float32)
    col = lax.rem(lax.broadcasted_iota(jnp.int32, (rows, chans), 0), width)
    left = jnp.where(col == 0, 0.0, pltpu.roll(wide[:, :chans], 1, 0))
    right = jnp.where(col == width - 1, 0.0, pltpu.roll(wide[:, 2 * chans :], rows - 1, 0))
    return wide[:, chans : 2 * chans] + left + right


def attend(normed, resid, qkv_weight, out_weight, mask):
    nframes, cells, chans = normed.shape
    mine = resid.shape[0]
    head_dim = chans // HEADS
    keys = nframes * TILE
    asks = mine * TILE
    query = jnp.dot(
        normed[:mine].reshape(mine * cells, chans), qkv_weight[:, :chans], preferred_element_type=jnp.float32
    ).reshape(mine, cells, chans)
    kv = jnp.dot(
        normed.reshape(nframes * cells, chans), qkv_weight[:, chans:], preferred_element_type=jnp.float32
    ).reshape(nframes, cells, 2 * chans)
    heads_of = lax.broadcasted_iota(jnp.int32, (asks, chans), 1) // head_dim
    mask = mask[:asks]
    outs, kept = [], []
    for j in range(0, cells, TILE):
        part = query[:, j : j + TILE].reshape(asks, chans).astype(jnp.bfloat16)
        part = part * jnp.bfloat16(1.0 / head_dim**0.5)
        pair = kv[:, j : j + TILE].reshape(keys, 2 * chans).astype(jnp.bfloat16)
        key_part, value = pair[:, :chans], pair[:, chans:]
        with_ones = jnp.concatenate([value, jnp.ones_like(value)], axis=1)
        picked = jnp.concatenate(
            [jnp.where(heads_of == h, part, jnp.zeros_like(part)) for h in range(HEADS)], axis=0
        )
        scores = lax.dot_general(
            picked, key_part, (((1,), (1,)), ((), ())), preferred_element_type=jnp.float32
        )
        scores = (scores.reshape(HEADS, asks, keys) + mask).reshape(HEADS * asks, keys)
        top = jnp.max(scores, axis=-1, keepdims=True)
        expd = jnp.exp((scores - top).astype(jnp.bfloat16))
        both = jnp.dot(expd, with_ones, preferred_element_type=jnp.float32)
        num, den = both[:asks, :chans], both[:asks, chans:]
        for h in range(1, HEADS):
            piece = both[h * asks : (h + 1) * asks]
            own = heads_of == h
            num = jnp.where(own, piece[:, :chans], num)
            den = jnp.where(own, piece[:, chans:], den)
        outs.append((num / den).astype(jnp.bfloat16))
        kept.append(resid[:, j : j + TILE].reshape(asks, chans))
    attended = jnp.concatenate(outs, axis=0)
    out = jnp.concatenate(kept, axis=0) + jnp.dot(attended, out_weight, preferred_element_type=jnp.float32)
    parts = [out[g * asks : (g + 1) * asks].reshape(mine, TILE, chans) for g in range(cells // TILE)]
    return jnp.concatenate(parts, axis=1)


def block_kernel(
    peers, spaces,
    x_ref, boundary_ref, w1_ref, w2_ref, gain_hbm, qkv_hbm, outw_hbm, o_ref,
    xpad, hpad, rbuf, nbuf, nall, rsib, abuf, taps_ref, quad, qbuf, bnd, gain_ref, qkv_ref, outw_ref, mask_ref,
    x_sem, w_sem, b_sem, p_sem, halo_send, halo_recv, there_send, there_recv, back_send, back_recv, own_sem, share_send, share_recv,
):
    nloc, rows, width, chans = x_ref.shape
    coarse = boundary_ref.shape[0]
    nframes = nloc * peers
    half = width // 2
    me = lax.axis_index("tm")
    place = lax.axis_index("space")
    last = spaces - 1
    core = lax.rem(me, 2)
    sibling = me + 1 - 2 * core
    across = lax.rem(me + 2, peers)
    crossed = lax.rem(sibling + 2, peers)

    batches = [pl.ds(0, 1), pl.ds(1, 2), pl.ds(3, nloc - 3)]

    def load(i):
        frames = batches[i]
        return pltpu.make_async_copy(x_ref.at[frames], xpad.at[frames, pl.ds(2, rows)], x_sem.at[i])

    weights = [
        pltpu.make_async_copy(ref, taps_ref.at[which], w_sem.at[which]) for which, ref in enumerate((w1_ref, w2_ref))
    ]
    edges = pltpu.make_async_copy(boundary_ref, bnd, b_sem)
    gains = pltpu.make_async_copy(gain_hbm, gain_ref, p_sem.at[2])
    projections = [
        pltpu.make_async_copy(qkv_hbm, qkv_ref, p_sem.at[0]),
        pltpu.make_async_copy(outw_hbm, outw_ref, p_sem.at[1]),
    ]
    for c in [load(0)] + weights + [gains, load(1), load(2)] + projections + [edges]:
        c.start()

    barrier = pltpu.get_barrier_semaphore()
    for k in (sibling, across, crossed):
        pl.semaphore_signal(barrier, inc=1, device_id={"tm": k}, device_id_type=MESH)

    @pl.when(place > 0)
    def _():
        pl.semaphore_signal(barrier, inc=1, device_id={"space": place - 1}, device_id_type=MESH)

    @pl.when(place < last)
    def _():
        pl.semaphore_signal(barrier, inc=1, device_id={"space": place + 1}, device_id_type=MESH)

    beside = jnp.where(place > 0, 1, 0) + jnp.where(place < last, 1, 0)
    pl.semaphore_wait(barrier, 3 + beside)

    def up(i):
        return pltpu.make_async_remote_copy(
            x_ref.at[:, i], xpad.at[:, rows + 2 + i], halo_send.at[0, i], halo_recv.at[0, i],
            device_id={"space": place - 1}, device_id_type=MESH,
        )

    def down(i):
        return pltpu.make_async_remote_copy(
            x_ref.at[:, rows - 1 - i], xpad.at[:, 1 - i], halo_send.at[1, i], halo_recv.at[1, i],
            device_id={"space": place + 1}, device_id_type=MESH,
        )

    for i in range(2):

        @pl.when(place > 0)
        def _(i=i):
            up(i).start()

        @pl.when(place < last)
        def _(i=i):
            down(i).start()

    row_id = lax.broadcasted_iota(jnp.int32, mask_ref.shape, 0)
    col_id = lax.broadcasted_iota(jnp.int32, mask_ref.shape, 1)
    mask_ref[...] = jnp.where(lax.rem(row_id, TILE) == lax.rem(col_id, TILE), 0.0, -1e30)
    def strip(frame, side):
        scaled = (me * nloc + frame) * (coarse - 1)
        lower = scaled // (nframes - 1)
        upper = jnp.minimum(lower + 1, coarse - 1)
        frac = (scaled - lower * (nframes - 1)).astype(jnp.float32) / float(nframes - 1)
        low, high = bnd[lower, side].astype(jnp.float32), bnd[upper, side].astype(jnp.float32)
        return ((1.0 - frac) * low + frac * high).astype(jnp.bfloat16)

    def kernel_of(which):
        return jnp.concatenate(
            [jnp.concatenate([taps_ref[which, dy, dx] for dx in range(3)], axis=1) for dy in range(3)], axis=0
        )

    def stacked(ref, frames, which):
        return jnp.concatenate([ref[frames, r].reshape(-1, chans) for r in which], axis=0)

    def hidden_rows(frames, which):
        taps = [stacked(xpad, frames, [r + dy for r in which]) for dy in range(3)]
        first = conv_taps(taps, kernel_of(0), width)
        act = (first / (1.0 + jnp.exp(-first))).astype(jnp.bfloat16)
        n = act.shape[0] // len(which)
        for i, r in enumerate(which):
            hpad[frames, r] = act[i * n : (i + 1) * n].reshape(n // width, width, chans)

    def resid_rows(frames, which, slot):
        taps = [stacked(hpad, frames, [r + dy for r in which]) for dy in range(3)]
        second = conv_taps(taps, kernel_of(1), width)
        before = stacked(xpad, frames, [r + 2 for r in which])
        resid = (before.astype(jnp.float32) + second).astype(jnp.bfloat16)
        wide = resid.astype(jnp.float32)
        normed = norm(wide)
        n = wide.shape[0] // len(which)
        for i in range(len(which)):
            for ref, v in ((rbuf, resid), (nbuf, normed)):
                v = v[i * n : (i + 1) * n].reshape(n // width, width, chans)
                ref[slot + i, 0, frames] = v[:, :half]
                ref[slot + i, 1, frames] = v[:, half:]

    def piece(slot, frames, begin, size, unit, k):
        side = core if k == 2 else 1 - core
        here = pl.ds(begin, size)
        src = (rbuf if k == 1 else nbuf).at[slot, side, frames, here]
        dst = rsib.at[slot, frames, here] if k == 1 else nall.at[slot, max(k - 1, 0), frames, here]
        return pltpu.make_async_remote_copy(
            src, dst, there_send.at[unit, k], there_recv.at[unit, k],
            device_id={"tm": sibling if k < 2 else crossed if k == 3 else across}, device_id_type=MESH,
        )

    every = pl.ds(0, nloc)
    early = [functools.partial(piece, 0, frames, 0, half, i) for i, frames in enumerate(batches)]

    def whole(slot):
        return functools.partial(piece, slot, every, 0, half, len(early) + slot - 2)

    starts = [sum(TAIL[:i]) for i in range(len(TAIL))]
    late = [
        functools.partial(piece, rows - 1, every, at, size, len(early) + rows - 3 + i)
        for i, (at, size) in enumerate(zip(starts, TAIL))
    ]

    group = (me, sibling, across, crossed)
    quarter = width // peers

    def share(k):
        to = group[k]
        begin = pl.multiple_of(lax.rem(to, 2) * quarter, quarter)
        return pltpu.make_async_remote_copy(
            rbuf.at[SHARED, to // 2, :, pl.ds(begin, quarter)], quad.at[k - 1],
            share_send.at[0, k - 1], share_recv.at[0, k - 1], device_id={"tm": to}, device_id_type=MESH,
        )

    def reply(k):
        cols = pl.ds(pl.multiple_of(me * quarter, quarter), quarter)
        dst = o_ref.at[:, SHARED + 2, cols]
        if k == 0:
            return pltpu.make_async_copy(qbuf.at[0], dst, own_sem.at[rows - 2 + len(TAIL)])
        return pltpu.make_async_remote_copy(
            qbuf.at[k], dst, share_send.at[1, k - 1], share_recv.at[1, k - 1],
            device_id={"tm": group[k]}, device_id_type=MESH,
        )

    def norm(wide):
        mean_sq = jnp.mean(wide * wide, axis=-1, keepdims=True)
        return (wide * lax.rsqrt(mean_sq + 1e-06) * gain_ref[...]).astype(jnp.bfloat16)

    def send(unit):
        for k in (2, 3, 0, 1):
            unit(k).start()

    weights[0].wait()
    for i, frames in enumerate(batches):
        load(i).wait()
        hidden_rows(frames, [2, 3, 4])
        if i == 0:
            weights[1].wait()
            gains.wait()
        resid_rows(frames, [2], 0)
        for k in (2, 3, 0, 1):
            early[i](k).start()
    hidden_rows(every, [5])
    resid_rows(every, [3], 1)
    for k in (2, 3, 1):
        share(k).start()
    hidden_rows(every, [6, 7])
    resid_rows(every, [4, 5], 2)
    send(whole(2))
    send(whole(3))

    for c in projections + [edges]:
        c.wait()

    def near_pair():
        @pl.when(place > 0)
        def _():
            down(0).wait_recv()

        @pl.when(place == 0)
        def _():
            for f in range(nloc):
                edge = strip(f, 0)
                xpad[f, 0] = edge
                xpad[f, 1] = edge

        @pl.when(place < last)
        def _():
            up(0).wait_recv()

        @pl.when(place == last)
        def _():
            for f in range(nloc):
                edge = strip(f, 1)
                xpad[f, rows + 2] = edge
                xpad[f, rows + 3] = edge

        hidden_rows(every, [1, rows])
        resid_rows(every, [1, rows - 2], 4)
        send(whole(4))
        send(whole(5))

    def edge_pair():

        @pl.when(place > 0)
        def _():
            down(1).wait_recv()

        @pl.when(place < last)
        def _():
            up(1).wait_recv()

        hidden_rows(every, [0, rows + 1])

        @pl.when(place == 0)
        def _():
            hpad[:, 0] = xpad[:, 1]

        @pl.when(place == last)
        def _():
            hpad[:, rows + 1] = xpad[:, rows + 2]

        resid_rows(every, [0, rows - 1], 6)
        send(whole(6))
        for unit in late:
            send(unit)
        for k in (2, 3, 1, 0):
            reply(k).start()

    def row_of(slot):
        k = slot - 4
        far = lax.rem(k + 4, 2)
        outer = (1 - k // 2) * (1 - far) + (rows - 2 + k // 2) * far
        return jnp.where(slot < 4, slot + 2, outer)

    def results(slot, row, begin, size, unit):
        here = pl.ds(begin, size)
        cols = pl.ds(pl.multiple_of(core * half + begin, size), size)
        mine = pltpu.make_async_copy(abuf.at[slot, pl.ds(0, nloc), here], o_ref.at[:, row, cols], own_sem.at[unit])
        theirs = pltpu.make_async_remote_copy(
            abuf.at[slot, pl.ds(nloc, nloc), here], o_ref.at[:, row, cols],
            back_send.at[unit], back_recv.at[unit], device_id={"tm": sibling}, device_id_type=MESH,
        )
        return mine, theirs

    def consume(slot, row, begin, size, unit):
        here = pl.ds(begin, size)
        normed = jnp.concatenate(
            [nbuf[slot, core, :, here, :], nall[slot, :, :, here, :].reshape(3 * nloc, size, chans)], axis=0
        )
        resid = jnp.concatenate([rbuf[slot, core, :, here, :], rsib[slot, :, here, :]], axis=0).astype(jnp.float32)
        out = attend(normed, resid, qkv_ref[...], outw_ref[...], mask_ref[...])
        abuf[slot, :, here, :] = out.astype(jnp.bfloat16)
        mine, theirs = results(slot, row, begin, size, unit)
        theirs.start()
        mine.start()

    def shared_row():
        for k in (1, 2, 3):
            share(k).wait_recv()
        begin = pl.multiple_of(core * quarter, quarter)
        own = rbuf[SHARED, me // 2, :, pl.ds(begin, quarter), :]
        resid = jnp.concatenate([own, quad[...].reshape(3 * nloc, quarter, chans)], axis=0).astype(jnp.float32)
        normed = norm(resid.reshape(nframes * quarter, chans)).reshape(nframes, quarter, chans)
        out = attend(normed, resid, qkv_ref[...], outw_ref[...], mask_ref[...])
        qbuf[...] = out.astype(jnp.bfloat16).reshape(peers, nloc, quarter, chans)

    for unit in early:
        for k in range(4):
            unit(k).wait_recv()

    def slot_of(s):
        return s + jnp.where(s >= SHARED, 1, 0)

    def step(s, carry):
        slot = slot_of(s)

        @pl.when(s > 0)
        def _():
            for k in range(4):
                whole(slot)(k).wait_recv()

        consume(slot, row_of(slot), 0, half, s)

        @pl.when(s == 0)
        def _():
            shared_row()
            near_pair()

        @pl.when(s == 2)
        def _():
            edge_pair()

        return carry

    lax.fori_loop(0, rows - 2, step, 0)
    for i, unit in enumerate(late):
        for k in range(4):
            unit(k).wait_recv()
        consume(rows - 1, rows - 1, starts[i], TAIL[i], rows - 2 + i)

    @pl.when(place > 0)
    def _():
        up(0).wait_send()
        up(1).wait_send()

    @pl.when(place < last)
    def _():
        down(0).wait_send()
        down(1).wait_send()

    for unit in early + late:
        for k in range(4):
            unit(k).wait_send()

    def drain(slot, carry):
        for k in range(4):
            whole(slot)(k).wait_send()
        return carry

    lax.fori_loop(2, rows - 1, drain, 0)
    for k in (1, 2, 3):
        share(k).wait_send()
        reply(k).wait()
    reply(0).wait()

    def settle(s, carry):
        for c in results(slot_of(s), row_of(slot_of(s)), 0, half, s):
            c.wait()
        return carry

    lax.fori_loop(0, rows - 2, settle, 0)
    for i in range(len(TAIL)):
        for c in results(rows - 1, rows - 1, starts[i], TAIL[i], rows - 2 + i):
            c.wait()


def on_device(frames_in, boundary, conv_first, conv_second, norm_gain, qkv_weight, out_weight):
    nloc, rows, width, chans = frames_in.shape
    peers = lax.axis_size("tm")
    spaces = lax.axis_size("space")
    nframes = nloc * peers
    half = width // 2
    units = 3 + rows - 3 + len(TAIL)
    hbm = pl.BlockSpec(memory_space=pl.ANY)
    bf16 = jnp.bfloat16
    dma = pltpu.SemaphoreType.DMA
    return pl.pallas_call(
        functools.partial(block_kernel, peers, spaces),
        out_shape=pltpu.VMEM(frames_in.shape, frames_in.dtype),
        in_specs=[hbm] * 7,
        out_specs=hbm,
        scratch_shapes=[
            pltpu.VMEM((nloc, rows + 4, width, chans), bf16),
            pltpu.VMEM((nloc, rows + 2, width, chans), bf16),
            pltpu.VMEM((rows, 2, nloc, half, chans), bf16),
            pltpu.VMEM((rows, 2, nloc, half, chans), bf16),
            pltpu.VMEM((rows, peers - 1, nloc, half, chans), bf16),
            pltpu.VMEM((rows, nloc, half, chans), bf16),
            pltpu.VMEM((rows, 2 * nloc, half, chans), bf16),
            pltpu.VMEM((2, *conv_first.shape), bf16),
            pltpu.VMEM((peers - 1, nloc, width // peers, chans), bf16),
            pltpu.VMEM((peers, nloc, width // peers, chans), bf16),
            pltpu.VMEM(boundary.shape, bf16),
            pltpu.VMEM((1, chans), jnp.float32),
            pltpu.VMEM(qkv_weight.shape, bf16),
            pltpu.VMEM(out_weight.shape, bf16),
            pltpu.VMEM((nframes * TILE, nframes * TILE), jnp.float32),
            dma((3,)), dma((2,)), dma, dma((3,)), dma((2, 2)), dma((2, 2)),
            dma((units, 4)), dma((units, 4)),
            dma((rows - 2 + len(TAIL),)), dma((rows - 2 + len(TAIL),)), dma((rows - 1 + len(TAIL),)),
            dma((2, 3)), dma((2, 3)),
        ],
        compiler_params=pltpu.CompilerParams(
            collective_id=0, has_side_effects=True, vmem_limit_bytes=54 * 1024 * 1024
        ),
        name="denoise",
    )(frames_in, boundary, conv_first, conv_second, norm_gain.reshape(1, chans), qkv_weight, out_weight)


def solution(mesh):
    placed = (P("tm", "space", None, None), P(), P(), P(), P(), P(), P())
    return jax.shard_map(
        on_device,
        mesh=mesh,
        in_specs=placed,
        out_specs=P("tm", "space", None, None),
        check_vma=False,
    )
```

```python
import functools

import jax
import jax.numpy as jnp
from jax import lax
from jax.experimental import pallas as pl
from jax.experimental.pallas import tpu as pltpu
from jax.sharding import PartitionSpec as P

HEADS = 8
MESH = pl.DeviceIdType.MESH
TILE = 8
TAIL = (32, 32)
SHARED = 1


def conv_taps(taps, weight, width):
    cells = jnp.concatenate(taps, axis=1)
    rows = cells.shape[0]
    chans = weight.shape[1] // 3
    wide = jnp.dot(cells, weight, preferred_element_type=jnp.float32)
    col = lax.rem(lax.broadcasted_iota(jnp.int32, (rows, chans), 0), width)
    left = jnp.where(col == 0, 0.0, pltpu.roll(wide[:, :chans], 1, 0))
    right = jnp.where(col == width - 1, 0.0, pltpu.roll(wide[:, 2 * chans :], rows - 1, 0))
    return wide[:, chans : 2 * chans] + left + right


def attend(normed, resid, qkv_weight, out_weight, mask):
    nframes, cells, chans = normed.shape
    mine = resid.shape[0]
    head_dim = chans // HEADS
    keys = nframes * TILE
    asks = mine * TILE
    query = jnp.dot(
        normed[:mine].reshape(mine * cells, chans), qkv_weight[:, :chans], preferred_element_type=jnp.float32
    ).reshape(mine, cells, chans)
    kv = jnp.dot(
        normed.reshape(nframes * cells, chans), qkv_weight[:, chans:], preferred_element_type=jnp.float32
    ).reshape(nframes, cells, 2 * chans)
    heads_of = lax.broadcasted_iota(jnp.int32, (asks, chans), 1) // head_dim
    mask = mask[:asks]
    outs, kept = [], []
    for j in range(0, cells, TILE):
        part = query[:, j : j + TILE].reshape(asks, chans).astype(jnp.bfloat16)
        part = part * jnp.bfloat16(1.0 / head_dim**0.5)
        pair = kv[:, j : j + TILE].reshape(keys, 2 * chans).astype(jnp.bfloat16)
        key_part, value = pair[:, :chans], pair[:, chans:]
        with_ones = jnp.concatenate([value, jnp.ones_like(value)], axis=1)
        picked = jnp.concatenate(
            [jnp.where(heads_of == h, part, jnp.zeros_like(part)) for h in range(HEADS)], axis=0
        )
        scores = lax.dot_general(
            picked, key_part, (((1,), (1,)), ((), ())), preferred_element_type=jnp.float32
        )
        scores = (scores.reshape(HEADS, asks, keys) + mask).reshape(HEADS * asks, keys)
        top = jnp.max(scores, axis=-1, keepdims=True)
        expd = jnp.exp((scores - top).astype(jnp.bfloat16))
        both = jnp.dot(expd, with_ones, preferred_element_type=jnp.float32)
        num, den = both[:asks, :chans], both[:asks, chans:]
        for h in range(1, HEADS):
            piece = both[h * asks : (h + 1) * asks]
            own = heads_of == h
            num = jnp.where(own, piece[:, :chans], num)
            den = jnp.where(own, piece[:, chans:], den)
        outs.append((num / den).astype(jnp.bfloat16))
        kept.append(resid[:, j : j + TILE].reshape(asks, chans))
    attended = jnp.concatenate(outs, axis=0)
    out = jnp.concatenate(kept, axis=0) + jnp.dot(attended, out_weight, preferred_element_type=jnp.float32)
    parts = [out[g * asks : (g + 1) * asks].reshape(mine, TILE, chans) for g in range(cells // TILE)]
    return jnp.concatenate(parts, axis=1)


def block_kernel(
    peers, spaces,
    x_ref, boundary_ref, w1_ref, w2_ref, gain_hbm, qkv_hbm, outw_hbm, o_ref,
    xpad, hpad, rbuf, nbuf, nall, rsib, abuf, taps_ref, quad, qbuf, bnd, gain_ref, qkv_ref, outw_ref, mask_ref,
    x_sem, w_sem, b_sem, p_sem, halo_send, halo_recv, there_send, there_recv, back_send, back_recv, own_sem, share_send, share_recv,
):
    nloc, rows, width, chans = x_ref.shape
    coarse = boundary_ref.shape[0]
    nframes = nloc * peers
    half = width // 2
    me = lax.axis_index("tm")
    place = lax.axis_index("space")
    last = spaces - 1
    core = lax.rem(me, 2)
    sibling = me + 1 - 2 * core
    across = lax.rem(me + 2, peers)
    crossed = lax.rem(sibling + 2, peers)

    batches = [pl.ds(0, 1), pl.ds(1, 2), pl.ds(3, nloc - 3)]

    def load(i):
        frames = batches[i]
        return pltpu.make_async_copy(x_ref.at[frames], xpad.at[frames, pl.ds(2, rows)], x_sem.at[i])

    weights = [
        pltpu.make_async_copy(ref, taps_ref.at[which], w_sem.at[which]) for which, ref in enumerate((w1_ref, w2_ref))
    ]
    edges = pltpu.make_async_copy(boundary_ref, bnd, b_sem)
    gains = pltpu.make_async_copy(gain_hbm, gain_ref, p_sem.at[2])
    projections = [
        pltpu.make_async_copy(qkv_hbm, qkv_ref, p_sem.at[0]),
        pltpu.make_async_copy(outw_hbm, outw_ref, p_sem.at[1]),
    ]
    for c in [load(0)] + weights + [gains, load(1), load(2)] + projections + [edges]:
        c.start()

    barrier = pltpu.get_barrier_semaphore()
    for k in (sibling, across, crossed):
        pl.semaphore_signal(barrier, inc=1, device_id={"tm": k}, device_id_type=MESH)

    @pl.when(place > 0)
    def _():
        pl.semaphore_signal(barrier, inc=1, device_id={"space": place - 1}, device_id_type=MESH)

    @pl.when(place < last)
    def _():
        pl.semaphore_signal(barrier, inc=1, device_id={"space": place + 1}, device_id_type=MESH)

    beside = jnp.where(place > 0, 1, 0) + jnp.where(place < last, 1, 0)
    pl.semaphore_wait(barrier, 3 + beside)

    def up(i):
        return pltpu.make_async_remote_copy(
            x_ref.at[:, i], xpad.at[:, rows + 2 + i], halo_send.at[0, i], halo_recv.at[0, i],
            device_id={"space": place - 1}, device_id_type=MESH,
        )

    def down(i):
        return pltpu.make_async_remote_copy(
            x_ref.at[:, rows - 1 - i], xpad.at[:, 1 - i], halo_send.at[1, i], halo_recv.at[1, i],
            device_id={"space": place + 1}, device_id_type=MESH,
        )

    for i in range(2):

        @pl.when(place > 0)
        def _(i=i):
            up(i).start()

        @pl.when(place < last)
        def _(i=i):
            down(i).start()

    row_id = lax.broadcasted_iota(jnp.int32, mask_ref.shape, 0)
    col_id = lax.broadcasted_iota(jnp.int32, mask_ref.shape, 1)
    mask_ref[...] = jnp.where(lax.rem(row_id, TILE) == lax.rem(col_id, TILE), 0.0, -1e30)
    def strip(frame, side):
        scaled = (me * nloc + frame) * (coarse - 1)
        lower = scaled // (nframes - 1)
        upper = jnp.minimum(lower + 1, coarse - 1)
        frac = (scaled - lower * (nframes - 1)).astype(jnp.float32) / float(nframes - 1)
        low, high = bnd[lower, side].astype(jnp.float32), bnd[upper, side].astype(jnp.float32)
        return ((1.0 - frac) * low + frac * high).astype(jnp.bfloat16)

    def kernel_of(which):
        return jnp.concatenate(
            [jnp.concatenate([taps_ref[which, dy, dx] for dx in range(3)], axis=1) for dy in range(3)], axis=0
        )

    def stacked(ref, frames, which):
        return jnp.concatenate([ref[frames, r].reshape(-1, chans) for r in which], axis=0)

    def hidden_rows(frames, which):
        taps = [stacked(xpad, frames, [r + dy for r in which]) for dy in range(3)]
        first = conv_taps(taps, kernel_of(0), width)
        act = (first / (1.0 + jnp.exp(-first))).astype(jnp.bfloat16)
        n = act.shape[0] // len(which)
        for i, r in enumerate(which):
            hpad[frames, r] = act[i * n : (i + 1) * n].reshape(n // width, width, chans)

    def resid_rows(frames, which, slot):
        taps = [stacked(hpad, frames, [r + dy for r in which]) for dy in range(3)]
        second = conv_taps(taps, kernel_of(1), width)
        before = stacked(xpad, frames, [r + 2 for r in which])
        resid = (before.astype(jnp.float32) + second).astype(jnp.bfloat16)
        wide = resid.astype(jnp.float32)
        sent = [(rbuf, resid)] if slot == SHARED else [(rbuf, resid), (nbuf, norm(wide))]
        n = wide.shape[0] // len(which)
        for i in range(len(which)):
            for ref, v in sent:
                v = v[i * n : (i + 1) * n].reshape(n // width, width, chans)
                ref[slot + i, 0, frames] = v[:, :half]
                ref[slot + i, 1, frames] = v[:, half:]

    def piece(slot, frames, begin, size, unit, k):
        side = core if k == 2 else 1 - core
        here = pl.ds(begin, size)
        src = (rbuf if k == 1 else nbuf).at[slot, side, frames, here]
        dst = rsib.at[slot, frames, here] if k == 1 else nall.at[slot, max(k - 1, 0), frames, here]
        return pltpu.make_async_remote_copy(
            src, dst, there_send.at[unit, k], there_recv.at[unit, k],
            device_id={"tm": sibling if k < 2 else crossed if k == 3 else across}, device_id_type=MESH,
        )

    every = pl.ds(0, nloc)
    early = [functools.partial(piece, 0, frames, 0, half, i) for i, frames in enumerate(batches)]

    def whole(slot):
        return functools.partial(piece, slot, every, 0, half, len(early) + slot - 2)

    starts = [sum(TAIL[:i]) for i in range(len(TAIL))]
    late = [
        functools.partial(piece, rows - 1, every, at, size, len(early) + rows - 3 + i)
        for i, (at, size) in enumerate(zip(starts, TAIL))
    ]

    group = (me, sibling, across, crossed)
    quarter = width // peers

    def share(k):
        to = group[k]
        begin = pl.multiple_of(lax.rem(to, 2) * quarter, quarter)
        return pltpu.make_async_remote_copy(
            rbuf.at[SHARED, to // 2, :, pl.ds(begin, quarter)], quad.at[k - 1],
            share_send.at[0, k - 1], share_recv.at[0, k - 1], device_id={"tm": to}, device_id_type=MESH,
        )

    def reply(k):
        cols = pl.ds(pl.multiple_of(me * quarter, quarter), quarter)
        dst = o_ref.at[:, SHARED + 2, cols]
        if k == 0:
            return pltpu.make_async_copy(qbuf.at[0], dst, own_sem.at[rows - 2 + len(TAIL)])
        return pltpu.make_async_remote_copy(
            qbuf.at[k], dst, share_send.at[1, k - 1], share_recv.at[1, k - 1],
            device_id={"tm": group[k]}, device_id_type=MESH,
        )

    def norm(wide):
        mean_sq = jnp.mean(wide * wide, axis=-1, keepdims=True)
        return (wide * lax.rsqrt(mean_sq + 1e-06) * gain_ref[...]).astype(jnp.bfloat16)

    def send(unit):
        for k in (2, 3, 0, 1):
            unit(k).start()

    weights[0].wait()
    for i, frames in enumerate(batches):
        load(i).wait()
        hidden_rows(frames, [2, 3, 4])
        if i == 0:
            weights[1].wait()
            gains.wait()
        resid_rows(frames, [2], 0)
        for k in (2, 3, 0, 1):
            early[i](k).start()
    hidden_rows(every, [5])
    resid_rows(every, [3], 1)
    for k in (2, 3, 1):
        share(k).start()
    hidden_rows(every, [6, 7])
    resid_rows(every, [4, 5], 2)
    send(whole(2))
    send(whole(3))

    for c in projections + [edges]:
        c.wait()

    def near_pair():
        @pl.when(place > 0)
        def _():
            down(0).wait_recv()

        @pl.when(place == 0)
        def _():
            for f in range(nloc):
                edge = strip(f, 0)
                xpad[f, 0] = edge
                xpad[f, 1] = edge

        @pl.when(place < last)
        def _():
            up(0).wait_recv()

        @pl.when(place == last)
        def _():
            for f in range(nloc):
                edge = strip(f, 1)
                xpad[f, rows + 2] = edge
                xpad[f, rows + 3] = edge

        hidden_rows(every, [1, rows])
        resid_rows(every, [1, rows - 2], 4)
        send(whole(4))
        send(whole(5))

    def edge_pair():

        @pl.when(place > 0)
        def _():
            down(1).wait_recv()

        @pl.when(place < last)
        def _():
            up(1).wait_recv()

        hidden_rows(every, [0, rows + 1])

        @pl.when(place == 0)
        def _():
            hpad[:, 0] = xpad[:, 1]

        @pl.when(place == last)
        def _():
            hpad[:, rows + 1] = xpad[:, rows + 2]

        resid_rows(every, [0, rows - 1], 6)
        send(whole(6))
        for unit in late:
            send(unit)
        for k in (2, 3, 1, 0):
            reply(k).start()

    def row_of(slot):
        k = slot - 4
        far = lax.rem(k + 4, 2)
        outer = (1 - k // 2) * (1 - far) + (rows - 2 + k // 2) * far
        return jnp.where(slot < 4, slot + 2, outer)

    def results(slot, row, begin, size, unit):
        here = pl.ds(begin, size)
        cols = pl.ds(pl.multiple_of(core * half + begin, size), size)
        mine = pltpu.make_async_copy(abuf.at[slot, pl.ds(0, nloc), here], o_ref.at[:, row, cols], own_sem.at[unit])
        theirs = pltpu.make_async_remote_copy(
            abuf.at[slot, pl.ds(nloc, nloc), here], o_ref.at[:, row, cols],
            back_send.at[unit], back_recv.at[unit], device_id={"tm": sibling}, device_id_type=MESH,
        )
        return mine, theirs

    def consume(slot, row, begin, size, unit):
        here = pl.ds(begin, size)
        normed = jnp.concatenate(
            [nbuf[slot, core, :, here, :], nall[slot, :, :, here, :].reshape(3 * nloc, size, chans)], axis=0
        )
        resid = jnp.concatenate([rbuf[slot, core, :, here, :], rsib[slot, :, here, :]], axis=0).astype(jnp.float32)
        out = attend(normed, resid, qkv_ref[...], outw_ref[...], mask_ref[...])
        abuf[slot, :, here, :] = out.astype(jnp.bfloat16)
        mine, theirs = results(slot, row, begin, size, unit)
        theirs.start()
        mine.start()

    def shared_row():
        for k in (1, 2, 3):
            share(k).wait_recv()
        begin = pl.multiple_of(core * quarter, quarter)
        own = rbuf[SHARED, me // 2, :, pl.ds(begin, quarter), :]
        resid = jnp.concatenate([own, quad[...].reshape(3 * nloc, quarter, chans)], axis=0).astype(jnp.float32)
        normed = norm(resid.reshape(nframes * quarter, chans)).reshape(nframes, quarter, chans)
        out = attend(normed, resid, qkv_ref[...], outw_ref[...], mask_ref[...])
        qbuf[...] = out.astype(jnp.bfloat16).reshape(peers, nloc, quarter, chans)

    for unit in early:
        for k in range(4):
            unit(k).wait_recv()

    def slot_of(s):
        return s + jnp.where(s >= SHARED, 1, 0)

    def step(s, carry):
        slot = slot_of(s)

        @pl.when(s > 0)
        def _():
            for k in range(4):
                whole(slot)(k).wait_recv()

        consume(slot, row_of(slot), 0, half, s)

        @pl.when(s == 0)
        def _():
            shared_row()
            near_pair()

        @pl.when(s == 2)
        def _():
            edge_pair()

        return carry

    lax.fori_loop(0, rows - 2, step, 0)
    for i, unit in enumerate(late):
        for k in range(4):
            unit(k).wait_recv()
        consume(rows - 1, rows - 1, starts[i], TAIL[i], rows - 2 + i)

    @pl.when(place > 0)
    def _():
        up(0).wait_send()
        up(1).wait_send()

    @pl.when(place < last)
    def _():
        down(0).wait_send()
        down(1).wait_send()

    for unit in early + late:
        for k in range(4):
            unit(k).wait_send()

    def drain(slot, carry):
        for k in range(4):
            whole(slot)(k).wait_send()
        return carry

    lax.fori_loop(2, rows - 1, drain, 0)
    for k in (1, 2, 3):
        share(k).wait_send()
        reply(k).wait()
    reply(0).wait()

    def settle(s, carry):
        for c in results(slot_of(s), row_of(slot_of(s)), 0, half, s):
            c.wait()
        return carry

    lax.fori_loop(0, rows - 2, settle, 0)
    for i in range(len(TAIL)):
        for c in results(rows - 1, rows - 1, starts[i], TAIL[i], rows - 2 + i):
            c.wait()


def on_device(frames_in, boundary, conv_first, conv_second, norm_gain, qkv_weight, out_weight):
    nloc, rows, width, chans = frames_in.shape
    peers = lax.axis_size("tm")
    spaces = lax.axis_size("space")
    nframes = nloc * peers
    half = width // 2
    units = 3 + rows - 3 + len(TAIL)
    hbm = pl.BlockSpec(memory_space=pl.ANY)
    bf16 = jnp.bfloat16
    dma = pltpu.SemaphoreType.DMA
    return pl.pallas_call(
        functools.partial(block_kernel, peers, spaces),
        out_shape=pltpu.VMEM(frames_in.shape, frames_in.dtype),
        in_specs=[hbm] * 7,
        out_specs=hbm,
        scratch_shapes=[
            pltpu.VMEM((nloc, rows + 4, width, chans), bf16),
            pltpu.VMEM((nloc, rows + 2, width, chans), bf16),
            pltpu.VMEM((rows, 2, nloc, half, chans), bf16),
            pltpu.VMEM((rows, 2, nloc, half, chans), bf16),
            pltpu.VMEM((rows, peers - 1, nloc, half, chans), bf16),
            pltpu.VMEM((rows, nloc, half, chans), bf16),
            pltpu.VMEM((rows, 2 * nloc, half, chans), bf16),
            pltpu.VMEM((2, *conv_first.shape), bf16),
            pltpu.VMEM((peers - 1, nloc, width // peers, chans), bf16),
            pltpu.VMEM((peers, nloc, width // peers, chans), bf16),
            pltpu.VMEM(boundary.shape, bf16),
            pltpu.VMEM((1, chans), jnp.float32),
            pltpu.VMEM(qkv_weight.shape, bf16),
            pltpu.VMEM(out_weight.shape, bf16),
            pltpu.VMEM((nframes * TILE, nframes * TILE), jnp.float32),
            dma((3,)), dma((2,)), dma, dma((3,)), dma((2, 2)), dma((2, 2)),
            dma((units, 4)), dma((units, 4)),
            dma((rows - 2 + len(TAIL),)), dma((rows - 2 + len(TAIL),)), dma((rows - 1 + len(TAIL),)),
            dma((2, 3)), dma((2, 3)),
        ],
        compiler_params=pltpu.CompilerParams(
            collective_id=0, has_side_effects=True, vmem_limit_bytes=54 * 1024 * 1024
        ),
        name="denoise",
    )(frames_in, boundary, conv_first, conv_second, norm_gain.reshape(1, chans), qkv_weight, out_weight)


def solution(mesh):
    placed = (P("tm", "space", None, None), P(), P(), P(), P(), P(), P())
    return jax.shard_map(
        on_device,
        mesh=mesh,
        in_specs=placed,
        out_specs=P("tm", "space", None, None),
        check_vma=False,
    )
```
